32 devices in a mesh: grp: 4 (over z), blk: 8 (over y, x, core).
Axes of the slice: x: 2, y: 2, z: 4, core: 2. Of those that a mesh axis runs over, the one named last changes fastest.
Arguments:
- pair_repr: bfloat16 [128, 128, 128], P(('grp', 'blk')), may hold values from -6 to 6
- pair_mask: int32 [128, 128], P(('grp', 'blk')), may hold values 0 or 1
- chain_index: int32 [128], replicated, may hold values from 0 to 3, never falling along the last dimension, each value on 1 to 64 neighbouring positions
- entity_embed: float32 [2, 128], replicated, may hold values from -3 to 3
- input_gain: float32 [2, 128], replicated, may hold values from 0.5 to 1.5
- input_bias: float32 [2, 128], replicated, may hold values from -2 to 2
- left_weight: bfloat16 [2, 128, 256], replicated, may hold values from -0.5 to 0.5
- right_weight: bfloat16 [2, 128, 256], replicated, may hold values from -0.5 to 0.5
- gate_weight: bfloat16 [2, 128, 128], replicated, may hold values from -0.5 to 0.5
- output_gain: float32 [2, 128], replicated, may hold values from 0.5 to 1.5
- output_bias: float32 [2, 128], replicated, may hold values from -2 to 2
- output_weight: bfloat16 [2, 128, 128], replicated, may hold values from -0.5 to 0.5
Outputs:
- pair_out: bfloat16 [128, 128, 128], P(('grp', 'blk'))
The draws below stay inside these ranges and needn't reach their ends.
Inputs may be any that keep to these rules, and one draw needn't show every extreme that they name: `chain_index`: chain numbers never fall along the residues and every one of the 4 chains has at least one residue.
All inputs are finite; a program needn't handle non-finite values. No bound on the sum of `pair_mask` on one device may be relied on, other than what follows from the above.
Results may differ from the reference program's by a relative error of at most 0.0055.
Values may be sent and summed in bfloat16 or wider, within the bound.
No kernel may reach another device: no remote copies, remote signals or barrier semaphores. Data moves between devices by JAX's collectives and lax.ppermute only.
A program may use at most 64 MiB of HBM per device.

```python
import math
import jax
import jax.numpy as jnp
import numpy as np
from jax import lax

CHAN = 128
HIDDEN_SIZE = 128
CHAINS = 4
N_RES = 128


def with_ends(values, stream_key, low, high):
    longest = values.shape.index(max(values.shape))
    spots = []
    for shift in (0, 1):
        where = [jax.random.randint(jax.random.fold_in(stream_key, axis), (), 0, length) for axis, length in enumerate(values.shape)]
        where[longest] = (where[longest] + shift) % values.shape[longest]
        spots.append(tuple(where))
    return values.at[spots[0]].set(low).at[spots[1]].set(high)


def block_scale(own_key, shape, cuts, least, high):
    def one(dim, shards_of):
        draws = jax.random.uniform(jax.random.fold_in(jax.random.fold_in(own_key, 6), dim), (shards_of,), jnp.float32, least / len(cuts), high / len(cuts))
        return jnp.repeat(jnp.exp(draws), shape[dim] // shards_of).reshape((-1,) + (1,) * (len(shape) - dim - 1))

    loudness = one(*cuts[0])
    for cut in cuts[1:]:
        loudness = loudness * one(*cut)
    return loudness


def profile(amount, total, bound, slope):
    weights = [(1 << 20) // math.isqrt(standing ** slope) + 1 for standing in range(2, amount + 1)]
    surplus, given = total - bound - (amount - 1), [1] * (amount - 1)
    while surplus > 0:
        movable = [i for i in range(amount - 1) if given[i] < bound]
        mass, left = sum([weights[i] for i in movable]), surplus
        for i in movable:
            extra = min(bound - given[i], max(1, left * weights[i] // mass), surplus)
            given[i] = given[i] + extra
            surplus = surplus - extra
    return np.array([bound] + given)


def uneven_parts(own_key, number_of, total, most, lean):
    if number_of == 2:
        one = jax.random.randint(own_key, (), max(1, total - most), min(most, total - 1) + 1)
        return jnp.stack([one, total - one])
    sizes = jnp.asarray(profile(number_of, total, most, lean), jnp.int32)
    couples = (number_of - 1) // 2
    source_of, sink = sizes[1:1 + 2 * couples:2], sizes[2:2 + 2 * couples:2]
    margin = jnp.minimum(source_of - 1, most - sink)
    moved = jax.random.randint(jax.random.fold_in(own_key, 1), (couples,), 0, 1 << 20) % (margin + 1)
    sizes = sizes.at[1:1 + 2 * couples:2].set(source_of - moved).at[2:2 + 2 * couples:2].set(sink + moved)
    return sizes[jax.random.permutation(jax.random.fold_in(own_key, 2), number_of)]


def scatter_about(own_key, shape, width, limit, cuts=(), dtype=jnp.bfloat16):
    loudness = block_scale(own_key, shape, cuts, -0.22, 0.18) if cuts else 1.0
    entries = jax.random.normal(own_key, shape, jnp.float32) * width * loudness
    return jnp.minimum(jnp.maximum(entries, -limit), limit).astype(dtype)


def setup_inputs(seed: int = 0) -> dict:
    arg_keys = jax.random.split(jax.random.key(seed), 13)
    pair_repr = scatter_about(arg_keys[0], (N_RES, N_RES, CHAN), 1.0, 6.0, ((0, 32),))
    pair_mask = with_ends((jax.random.randint(arg_keys[1], (N_RES, N_RES), 0, 8) < 7).astype(jnp.int32), jax.random.fold_in(arg_keys[1], 1), 0, 1)
    chain_index = jnp.searchsorted(jnp.cumsum(uneven_parts(arg_keys[2], CHAINS, N_RES, N_RES // 2, 2)), jnp.arange(N_RES), side="right").astype(jnp.int32)
    entity_embed = scatter_about(arg_keys[3], (2, CHAN), 0.5, 3.0, (), jnp.float32)
    input_gain = jnp.clip(1.0 + 0.1 * jax.random.normal(arg_keys[4], (2, CHAN), jnp.float32), 0.5, 1.5)
    input_bias = scatter_about(arg_keys[5], (2, CHAN), 0.3, 2.0, (), jnp.float32)
    left_weight = scatter_about(arg_keys[6], (2, CHAN, 2 * HIDDEN_SIZE), CHAN ** -0.5, 0.5)
    right_weight = scatter_about(arg_keys[7], (2, CHAN, 2 * HIDDEN_SIZE), CHAN ** -0.5, 0.5)
    gate_weight = scatter_about(arg_keys[8], (2, CHAN, CHAN), CHAN ** -0.5, 0.5)
    output_gain = jnp.clip(1.0 + 0.1 * jax.random.normal(arg_keys[9], (2, HIDDEN_SIZE), jnp.float32), 0.5, 1.5)
    output_bias = scatter_about(arg_keys[10], (2, HIDDEN_SIZE), 0.3, 2.0, (), jnp.float32)
    output_weight = scatter_about(arg_keys[11], (2, HIDDEN_SIZE, CHAN), HIDDEN_SIZE ** -0.5, 0.5)
    return {"pair_repr": pair_repr, "pair_mask": pair_mask, "chain_index": chain_index, "entity_embed": entity_embed, "input_gain": input_gain, "input_bias": input_bias, "left_weight": left_weight, "right_weight": right_weight, "gate_weight": gate_weight, "output_gain": output_gain, "output_bias": output_bias, "output_weight": output_weight}


def normalize(values, gain_vector, bias_vector, along):
    average = lax.optimization_barrier(jnp.mean(values, axis=along, keepdims=True))
    centered = values - average
    variance = lax.optimization_barrier(jnp.mean(centered * centered, axis=along, keepdims=True))
    return centered * lax.rsqrt(variance + 1e-05) * gain_vector + bias_vector

def edge_block(flat, weight, mask_column, row_block):
    projected = jnp.dot(flat, weight, preferred_element_type=jnp.float32)
    values = jax.nn.sigmoid(projected[:, :HIDDEN_SIZE]) * projected[:, HIDDEN_SIZE:] * mask_column
    return values.astype(jnp.bfloat16).reshape(row_block, N_RES, HIDDEN_SIZE)

def reference(pair_repr, pair_mask, chain_index, entity_embed, input_gain, input_bias, left_weight, right_weight, gate_weight, output_gain, output_bias, output_weight):
    row_block = math.gcd(N_RES, 64)
    block_total = N_RES // row_block
    chain_blocks = chain_index.reshape(block_total, row_block)
    mask_blocks = pair_mask.reshape(block_total, row_block, N_RES)
    forms = ['hik,hjk->hij', 'hki,hkj->hij']
    group = 8
    base = pair_repr
    for block_index in range(2):

        def state_of(block, chains):
            values = block.astype(jnp.float32)
            if block_index == 0:
                same_chain = chains[:, None] == chain_index[None, :]
                values = values + jnp.where(same_chain[:, :, None], entity_embed[1], entity_embed[0])
            return values.reshape(row_block * N_RES, CHAN)

        def normed_of(values):
            return normalize(values, input_gain[block_index], input_bias[block_index], 1).astype(jnp.bfloat16)

        def edges(items):
            block, chains, mask = items
            normed = normed_of(state_of(block, chains))
            mask_column = mask.astype(jnp.float32).reshape(row_block * N_RES, 1)
            left_part = edge_block(normed, left_weight[block_index], mask_column, row_block)
            right_part = edge_block(normed, right_weight[block_index], mask_column, row_block)
            return (left_part, right_part)
        base_blocks = base.reshape(block_total, row_block, N_RES, CHAN)
        left_blocks, right_blocks = lax.map(edges, (base_blocks, chain_blocks, mask_blocks))
        left_plane = left_blocks.reshape(N_RES, N_RES, HIDDEN_SIZE).transpose(2, 0, 1)
        right_plane = right_blocks.reshape(N_RES, N_RES, HIDDEN_SIZE).transpose(2, 0, 1)
        form = forms[block_index]

        def contract(pieces):
            return jnp.einsum(form, pieces[0].astype(jnp.float32), pieces[1].astype(jnp.float32)).astype(jnp.bfloat16)
        product = lax.map(contract, (left_plane.reshape(HIDDEN_SIZE // group, group, N_RES, N_RES), right_plane.reshape(HIDDEN_SIZE // group, group, N_RES, N_RES)))
        product_blocks = product.reshape(HIDDEN_SIZE, block_total, row_block, N_RES).transpose(1, 0, 2, 3)

        def finish(items):
            block, chains, piece = items
            values = state_of(block, chains)
            normed = normed_of(values)
            gating = jax.nn.sigmoid(jnp.dot(normed, gate_weight[block_index], preferred_element_type=jnp.float32))
            flat_product = piece.reshape(HIDDEN_SIZE, row_block * N_RES).astype(jnp.float32)
            normed_out = normalize(flat_product, output_gain[block_index][:, None], output_bias[block_index][:, None], 0).astype(jnp.bfloat16)
            update = lax.dot_general(normed_out, output_weight[block_index], (((0,), (0,)), ((), ())), preferred_element_type=jnp.float32)
            return (values + gating * update).astype(jnp.bfloat16).reshape(row_block, N_RES, CHAN)
        stored = lax.map(finish, (base_blocks, chain_blocks, product_blocks))
        base = lax.optimization_barrier(stored.reshape(N_RES, N_RES, CHAN))
    return base
```

```python
import jax
import jax.numpy as jnp
from jax import lax
from jax.sharding import PartitionSpec as P


def normalize(values, gain_vector, bias_vector, along):
    average = jnp.mean(values, axis=along, keepdims=True)
    centered = values - average
    variance = jnp.mean(centered * centered, axis=along, keepdims=True)
    return centered * lax.rsqrt(variance + 1e-05) * gain_vector + bias_vector


def edge_values(normed, weight, mask_rows, hidden_count, row_count, columns):
    projected = lax.dot_general(
        weight, normed, (((0,), (1,)), ((), ())), preferred_element_type=jnp.float32
    )
    values = jax.nn.sigmoid(projected[:hidden_count]) * projected[hidden_count:] * mask_rows
    return values.astype(jnp.bfloat16).reshape(hidden_count, row_count, columns)


def to_planes(left_rows, right_rows, group_count, block_count):
    hidden_count, row_count, columns = left_rows.shape
    devices = group_count * block_count
    per_device = hidden_count // devices
    both = jnp.stack([left_rows, right_rows], axis=1).reshape(
        devices, per_device * 2 * row_count, columns
    )
    moved = lax.all_to_all(both, ("grp", "blk"), split_axis=0, concat_axis=0, tiled=True)
    planes = moved.reshape(devices, per_device, 2, row_count, columns).transpose(2, 1, 0, 3, 4)
    planes = planes.reshape(2, per_device, devices * row_count, columns)
    return planes[0], planes[1]


def to_rows(product, group_count, block_count, row_count):
    per_device, total_rows, columns = product.shape
    shaped = product.reshape(1, per_device, group_count * block_count, row_count, columns)
    returned = lax.all_to_all(shaped, ("grp", "blk"), split_axis=2, concat_axis=0, tiled=True)
    return returned.reshape(-1, row_count * columns)


def shards(
    pair_repr,
    pair_mask,
    chain_index,
    entity_embed,
    input_gain,
    input_bias,
    left_weight,
    right_weight,
    gate_weight,
    output_gain,
    output_bias,
    output_weight,
):
    row_count, columns, channels = pair_repr.shape
    hidden_count = output_weight.shape[1]
    group_count = lax.axis_size("grp")
    block_count = lax.axis_size("blk")
    first_row = lax.axis_index(("grp", "blk")) * row_count
    own_chain = lax.dynamic_slice_in_dim(chain_index, first_row, row_count)
    same_chain = own_chain[:, None] == chain_index[None, :]
    current = pair_repr.astype(jnp.float32) + jnp.where(
        same_chain[:, :, None], entity_embed[1], entity_embed[0]
    )
    current = current.reshape(row_count * columns, channels)
    mask_rows = pair_mask.astype(jnp.float32).reshape(1, row_count * columns)
    contractions = [(((2,), (2,)), ((0,), (0,))), (((1,), (1,)), ((0,), (0,)))]
    stored = None
    for block_index in range(2):
        normed = normalize(current, input_gain[block_index], input_bias[block_index], 1).astype(
            jnp.bfloat16
        )
        left_rows = edge_values(
            normed, left_weight[block_index], mask_rows, hidden_count, row_count, columns
        )
        right_rows = edge_values(
            normed, right_weight[block_index], mask_rows, hidden_count, row_count, columns
        )
        gating = jax.nn.sigmoid(
            jnp.dot(normed, gate_weight[block_index], preferred_element_type=jnp.float32)
        )
        left_plane, right_plane = to_planes(left_rows, right_rows, group_count, block_count)
        product = lax.dot_general(
            left_plane, right_plane, contractions[block_index], preferred_element_type=jnp.float32
        ).astype(jnp.bfloat16)
        returned = to_rows(product, group_count, block_count, row_count).astype(jnp.float32)
        normed_out = normalize(
            returned, output_gain[block_index][:, None], output_bias[block_index][:, None], 0
        ).astype(jnp.bfloat16)
        update = lax.dot_general(
            normed_out,
            output_weight[block_index],
            (((0,), (0,)), ((), ())),
            preferred_element_type=jnp.float32,
        )
        stored = (current + gating * update).astype(jnp.bfloat16)
        current = lax.optimization_barrier(stored).astype(jnp.float32)
    return stored.reshape(row_count, columns, channels)


def solution(mesh):
    placed = (
        P(("grp", "blk"), None, None),
        P(("grp", "blk"), None),
        P(),
        P(),
        P(),
        P(),
        P(),
        P(),
        P(),
        P(),
        P(),
        P(),
    )
    return jax.shard_map(
        shards, mesh=mesh, in_specs=placed, out_specs=P(("grp", "blk"), None, None), check_vma=False
    )
```

```python
import functools

import jax
import jax.numpy as jnp
from jax import lax
from jax.experimental import pallas as pl
from jax.experimental.pallas import tpu as pltpu
from jax.sharding import PartitionSpec as P

AXES = ("grp", "blk")
F32, BF16 = jnp.float32, jnp.bfloat16
ON_SUBLANES = (((0,), (0,)), ((), ()))
ON_LANES = (((1,), (1,)), ((), ()))
LANES = 128


def unit(size):
    down = lax.broadcasted_iota(jnp.int32, (size, size), 0)
    across = lax.broadcasted_iota(jnp.int32, (size, size), 1)
    return jnp.where(down == across, 1.0, 0.0).astype(BF16)


def as_columns(rows_ref, *rows):
    rows_ref[...] = jnp.zeros(rows_ref.shape, F32)
    for place, row in enumerate(rows):
        rows_ref[place : place + 1, :] = row
    turned = jnp.transpose(rows_ref[...])
    return [turned[:, place : place + 1] for place in range(len(rows))]


def normalize(values, gain, bias):
    average = jnp.mean(values, axis=0, keepdims=True)
    centered = values - average
    variance = jnp.mean(centered * centered, axis=0, keepdims=True)
    return centered * lax.rsqrt(variance + 1e-05) * gain + bias


def put(ref, first, count, stride, values):
    for part in range(ref.shape[0]):
        at = part * LANES
        ref[part, pl.ds(first, count, stride=stride), :] = values[:, at : at + LANES]


def take(ref, first, count, stride):
    rows = pl.ds(first, count, stride=stride)
    return jnp.concatenate([ref[part, rows, :] for part in range(ref.shape[0])], axis=1)


def widen(source, ref):
    for part in range(ref.shape[0]):
        ref[part] = source[:, part * LANES : (part + 1) * LANES].astype(F32)


def pack(ref, out):
    for part in range(ref.shape[0]):
        out[:, part * LANES : (part + 1) * LANES] = ref[part].astype(BF16)


def edges(normed_ref, sides, mask_ref, e32, out_ref):
    row_count, columns = mask_ref.shape
    hidden = e32.shape[1] // (2 * row_count)
    for row in range(row_count):
        lanes = pl.ds(row * columns, columns)
        mask = mask_ref[row : row + 1, :]
        for side, weight in enumerate(sides):
            projected = lax.dot_general(
                weight, normed_ref[:, lanes], ON_SUBLANES, preferred_element_type=F32
            )
            values = jax.nn.sigmoid(projected[:hidden]) * projected[hidden:] * mask
            put(e32, side * row_count + row, hidden, 2 * row_count, values)
    pack(e32, out_ref)


def gates(normed_ref, weight, out_ref):
    out_ref[...] = jax.nn.sigmoid(
        lax.dot_general(weight, normed_ref[...], ON_SUBLANES, preferred_element_type=F32)
    )


def start_kernel(
    pair_h, mask_h, chain_h, embed_h, gain_h, bias_h, gain_oh, bias_oh, left_h, right_h, gate_h,
    out, state, gating, mask_out, columns_out,
    pair, mask, chain, embed, gain, bias, gain_o, bias_o, left, right, gate,
    e32, normed, rows, arrived,
):
    moves = [
        pltpu.make_async_copy(source, target, arrived.at[place])
        for place, (source, target) in enumerate(
            [
                (pair_h, pair),
                (chain_h, chain),
                (embed_h, embed),
                (gain_h, gain),
                (bias_h, bias),
                (gain_oh, gain_o),
                (bias_oh, bias_o),
                (left_h.at[0], left),
                (mask_h, mask),
                (right_h.at[0], right),
                (gate_h.at[0], gate),
            ]
        )
    ]
    for move in moves:
        move.start()
    row_count, columns, channels = pair.shape
    first = lax.axis_index(AXES) * row_count
    one = unit(channels)
    for move in moves[1:7]:
        move.wait()
    other, same, gain_c, bias_c = as_columns(
        rows, embed[0:1, :], embed[1:2, :], gain[0:1, :], bias[0:1, :]
    )
    rows[0:8, :] = jnp.concatenate([gain_o[...], bias_o[...], gain[...], bias[...]])
    columns_out[...] = jnp.transpose(rows[...])
    chains = jnp.broadcast_to(chain[...].astype(F32), (row_count, chain.shape[1]))
    place = lax.broadcasted_iota(jnp.int32, chains.shape, 1)
    mine = first + lax.broadcasted_iota(jnp.int32, chains.shape, 0)
    own = jnp.sum(jnp.where(place == mine, chains, 0.0), axis=1, keepdims=True)
    alike = jnp.where(chains == own, 1.0, 0.0)
    moves[0].wait()
    for row in range(row_count):
        lanes = pl.ds(row * columns, columns)
        turned = lax.dot_general(one, pair[row], ON_LANES, preferred_element_type=F32)
        hit = jnp.broadcast_to(alike[row : row + 1, :], turned.shape) > 0.5
        values = turned + jnp.where(hit, same, other)
        state[:, lanes] = values
        normed[:, lanes] = normalize(values, gain_c, bias_c).astype(BF16)
    for move in moves[7:]:
        move.wait()
    mask_out[...] = mask[...].astype(F32)
    edges(normed, (left[...], right[...]), mask_out, e32, out)
    gates(normed, gate[...], gating)


def product_kernel(incoming, devices, x, out, x32, t32, o32):
    columns = x.shape[1]
    row_count = columns // devices
    per_device = x.shape[0] // (2 * columns)
    widen(x, x32)
    apart = per_device * 2 * row_count

    def block(channel, side, row):
        return take(x32, channel * 2 * row_count + side * row_count + row, devices, apart)

    for channel in range(per_device):
        left = jnp.concatenate([block(channel, 0, r) for r in range(row_count)]).astype(BF16)
        if incoming:
            right = jnp.concatenate([block(channel, 1, r) for r in range(row_count)])
            product = lax.dot_general(
                left, right.astype(BF16), ON_SUBLANES, preferred_element_type=F32
            )
            put(t32, 0, columns, 1, product)
            pieces = [take(t32, r, devices, row_count) for r in range(row_count)]
        else:
            for r in range(row_count):
                put(t32, r, devices, row_count, block(channel, 1, r))
            right = take(t32, 0, columns, 1).astype(BF16)
            product = lax.dot_general(left, right, ON_LANES, preferred_element_type=F32)
            pieces = [product[r * devices : (r + 1) * devices] for r in range(row_count)]
        for r in range(row_count):
            put(o32, channel * row_count + r, devices, per_device * row_count, pieces[r])
    pack(o32, out)


def finish(y, y32, normed, gain_c, bias_c, weight, columns):
    hidden, positions = normed.shape
    row_count = positions // columns
    widen(y, y32)
    for row in range(row_count):
        values = take(y32, row, hidden, row_count)
        normed[:, pl.ds(row * columns, columns)] = normalize(values, gain_c, bias_c).astype(BF16)
    return lax.dot_general(weight, normed[...], ON_SUBLANES, preferred_element_type=F32)


def middle_kernel(
    y, state, gating, mask, turned, weight_o, left, right, gate,
    out, state_out, gating_out, y32, e32, normed,
):
    row_count, columns = mask.shape
    update = finish(y, y32, normed, turned[:, 0:1], turned[:, 2:3], weight_o[0], columns)
    state_out[...] = (state[...] + gating[...] * update).astype(BF16)
    for row in range(row_count):
        lanes = pl.ds(row * columns, columns)
        values = state_out[:, lanes].astype(F32)
        normed[:, lanes] = normalize(values, turned[:, 5:6], turned[:, 7:8]).astype(BF16)
    edges(normed, (left[1], right[1]), mask, e32, out)
    gates(normed, gate[1], gating_out)


def end_kernel(y, state, gating, turned, weight_o, out, y32, normed, ready, sent):
    row_count, columns, channels = out.shape
    update = finish(y, y32, normed, turned[:, 1:2], turned[:, 3:4], weight_o[1], columns)
    stored = (state[...].astype(F32) + gating[...] * update).astype(BF16)
    one = unit(LANES)
    moves = []
    for row in range(row_count):
        for part in range(columns // LANES):
            at = row * columns + part * LANES
            flat = lax.dot_general(
                one, stored[:, at : at + LANES], ON_LANES, preferred_element_type=F32
            )
            ready[row, pl.ds(part * LANES, LANES), :] = flat.astype(BF16)
        moves.append(pltpu.make_async_copy(ready.at[row], out.at[row], sent.at[row]))
        moves[-1].start()
    for move in moves:
        move.wait()


def call(kernel, shapes, scratch, semaphores=0, far_in=False, far_out=False):
    near = pl.BlockSpec(memory_space=pltpu.VMEM)
    far = pl.BlockSpec(memory_space=pltpu.HBM)

    def run(*operands):
        if far_in:
            operands = [pltpu.with_memory_space_constraint(o, pltpu.HBM) for o in operands]
        return pl.pallas_call(
            kernel,
            out_shape=[jax.ShapeDtypeStruct(*s) for s in shapes],
            in_specs=[far if far_in else near] * len(operands),
            out_specs=[far if far_out else near] * len(shapes),
            scratch_shapes=[pltpu.VMEM(*s) for s in scratch]
            + [pltpu.SemaphoreType.DMA((semaphores,))] * (semaphores > 0),
            compiler_params=pltpu.CompilerParams(vmem_limit_bytes=16 << 20),
        )(*operands)

    return run


def exchange(rows):
    devices = lax.axis_size(AXES[0]) * lax.axis_size(AXES[1])
    count, columns = rows.shape
    moved = lax.all_to_all(
        rows.reshape(devices, count // devices, columns),
        AXES,
        split_axis=0,
        concat_axis=0,
        tiled=True,
    )
    return moved.reshape(count, columns)


def shards(
    pair_repr,
    pair_mask,
    chain_index,
    entity_embed,
    input_gain,
    input_bias,
    left_weight,
    right_weight,
    gate_weight,
    output_gain,
    output_bias,
    output_weight,
):
    row_count, columns, channels = pair_repr.shape
    hidden = output_weight.shape[1]
    devices = lax.axis_size(AXES[0]) * lax.axis_size(AXES[1])
    positions = row_count * columns
    edge = (hidden * 2 * row_count, columns)
    prod = (hidden * row_count, columns)
    wide = (channels, positions)

    def tall(shape):
        return ((shape[1] // LANES, shape[0], LANES), F32)

    columnar = ((channels, 8), F32)
    weights = [left_weight.shape[1:], right_weight.shape[1:], gate_weight.shape[1:]]

    sent, state, gating, mask, turned = call(
        start_kernel,
        [(edge, BF16), (wide, F32), (wide, F32), (pair_mask.shape, F32), columnar],
        [(pair_repr.shape, BF16), (pair_mask.shape, jnp.int32), ((1, columns), jnp.int32)]
        + [((2, channels), F32)] * 5
        + [(shape, BF16) for shape in weights]
        + [tall(edge), (wide, BF16), ((8, channels), F32)],
        semaphores=11,
        far_in=True,
    )(
        pair_repr, pair_mask, chain_index.reshape(1, -1), entity_embed, input_gain, input_bias,
        output_gain, output_bias, left_weight, right_weight, gate_weight,
    )

    def product(rows, incoming):
        return call(
            functools.partial(product_kernel, incoming, devices),
            [(prod, BF16)],
            [tall(edge), tall((columns, columns)), tall(prod)],
        )(rows)[0]

    back = exchange(product(exchange(sent), False))
    sent, state, gating = call(
        middle_kernel,
        [(edge, BF16), (wide, BF16), (wide, F32)],
        [tall(prod), tall(edge), (wide, BF16)],
    )(back, state, gating, mask, turned, output_weight, left_weight, right_weight, gate_weight)
    back = exchange(product(exchange(sent), True))
    return call(
        end_kernel,
        [(pair_repr.shape, BF16)],
        [tall(prod), (wide, BF16), (pair_repr.shape, BF16)],
        semaphores=row_count,
        far_out=True,
    )(back, state, gating, turned, output_weight)[0]


def solution(mesh):
    rows = P(AXES, None)
    placed = (P(AXES, None, None), rows) + (P(),) * 10
    return jax.shard_map(
        shards, mesh=mesh, in_specs=placed, out_specs=P(AXES, None, None), check_vma=False
    )
```

```python
import functools

import jax
import jax.numpy as jnp
from jax import lax
from jax.experimental import pallas as pl
from jax.experimental.pallas import tpu as pltpu
from jax.sharding import PartitionSpec as P

AXES = ("grp", "blk")
F32, BF16 = jnp.float32, jnp.bfloat16
ON_SUBLANES = (((0,), (0,)), ((), ()))
ON_LANES = (((1,), (1,)), ((), ()))
LANES = 128


def unit(scale):
    down = lax.broadcasted_iota(jnp.int32, (LANES, LANES), 0)
    across = lax.broadcasted_iota(jnp.int32, (LANES, LANES), 1)
    return jnp.where(down == across, scale, 0.0).astype(BF16)


def turn(one, block):
    parts = [
        lax.dot_general(
            one, block[:, at : at + LANES], ON_LANES, preferred_element_type=F32
        ).astype(BF16)
        for at in range(0, block.shape[1], LANES)
    ]
    return jnp.concatenate(parts)


def turn_all(left, right, gate):
    parts = []
    for side in (left, right):
        hidden = side.shape[1] // 2
        parts += [side[:, :hidden] * 0.5, side[:, hidden:]]
    return jnp.transpose(jnp.concatenate(parts + [gate * 0.5], axis=1))


def spread(column):
    return jnp.broadcast_to(column, (column.shape[0], LANES))


def normalize(values, gain, bias):
    average = jnp.mean(values, axis=0, keepdims=True)
    centered = values - average
    variance = jnp.mean(centered * centered, axis=0, keepdims=True)
    return (centered * lax.rsqrt(variance + 1e-05) * gain + bias).astype(BF16)


def put(ref, first, count, stride, values):
    for part in range(ref.shape[0]):
        at = part * LANES
        ref[part, pl.ds(first, count, stride=stride), :] = values[:, at : at + LANES]


def take(ref, first, count, stride):
    rows = pl.ds(first, count, stride=stride)
    return jnp.concatenate([ref[part, rows, :] for part in range(ref.shape[0])], axis=1)


def widen(source, ref):
    for part in range(ref.shape[0]):
        ref[part] = source[:, part * LANES : (part + 1) * LANES].astype(F32)


def pack(ref, out):
    for part in range(ref.shape[0]):
        out[:, part * LANES : (part + 1) * LANES] = ref[part].astype(BF16)


def project(normed, weights, first, mask, e32, gating):
    row_count, columns = mask.shape
    hidden = e32.shape[1] // (2 * row_count)
    projected = jnp.dot(weights, normed, preferred_element_type=F32)
    for at in range(0, normed.shape[1], LANES):
        row, column = divmod(first + at, columns)
        block = projected[:, at : at + LANES]
        kept = mask[row : row + 1, column : column + LANES]
        for side in range(2):
            low = 2 * hidden * side
            values = block[low + hidden : low + 2 * hidden] * kept
            values = (jnp.tanh(block[low : low + hidden]) + 1.0) * values
            rows = pl.ds(side * row_count + row, hidden, stride=2 * row_count)
            e32[column // LANES, rows, :] = values
        gating[:, first + at : first + at + LANES] = jnp.tanh(block[4 * hidden :]) + 1.0


def start_kernel(
    pair_h, mask_h, chain_h, embed_h, gain_h, bias_h, gain_oh, bias_oh, left_h, right_h, gate_h,
    out, state, gating, mask_out, columns_out,
    pair, mask, chain, embed, gain, bias, gain_o, bias_o, left, right, gate,
    e32, rows, arrived,
):
    row_count, columns, channels = pair.shape
    wanted = [
        (pair_h, pair),
        (embed_h, embed),
        (gain_h, gain),
        (bias_h, bias),
        (gain_oh, gain_o),
        (bias_oh, bias_o),
        (chain_h, chain),
        (left_h.at[0], left),
        (right_h.at[0], right),
        (gate_h.at[0], gate),
        (mask_h, mask),
    ]
    moves = [
        pltpu.make_async_copy(source, target, arrived.at[place])
        for place, (source, target) in enumerate(wanted)
    ]
    for move in moves:
        move.start()
    first = lax.axis_index(AXES) * row_count
    one = unit(1.0)
    for move in moves[:7]:
        move.wait()
    rows[0:2, :] = gain_o[...]
    rows[2:4, :] = bias_o[...]
    rows[4:6, :] = gain[...]
    rows[6:8, :] = bias[...]
    turned = jnp.transpose(rows[...])
    columns_out[...] = turned
    gain_c, bias_c = spread(turned[:, 4:5]), spread(turned[:, 6:7])
    rows[0:2, :] = embed[...]
    turned = jnp.transpose(rows[...])
    other, same = spread(turned[:, 0:1]), spread(turned[:, 1:2])
    chains = jnp.broadcast_to(chain[...].astype(F32), (row_count, chain.shape[1]))
    place = lax.broadcasted_iota(jnp.int32, chains.shape, 1)
    mine = first + lax.broadcasted_iota(jnp.int32, chains.shape, 0)
    own = jnp.sum(jnp.where(place == mine, chains, 0.0), axis=1, keepdims=True)
    alike = jnp.where(chains == own, 1.0, 0.0)
    normed = []
    for begin in range(0, row_count * columns, LANES):
        row, column = divmod(begin, columns)
        values = lax.dot_general(
            one, pair[row, column : column + LANES, :], ON_LANES, preferred_element_type=F32
        )
        hit = jnp.broadcast_to(alike[row : row + 1, column : column + LANES], values.shape)
        values = values + jnp.where(hit > 0.5, same, other)
        state[:, begin : begin + LANES] = values
        normed.append(normalize(values, gain_c, bias_c))
    for move in moves[7:]:
        move.wait()
    mask_out[...] = mask[...].astype(F32) * 0.5
    weights = turn_all(left[...], right[...], gate[...])
    for place in range(0, len(normed), 2):
        pair_of = jnp.concatenate(normed[place : place + 2], axis=1)
        project(pair_of, weights, place * LANES, mask_out, e32, gating)
    pack(e32, out)


def apart(low, high, half):
    upper = lax.broadcasted_iota(jnp.int32, low.shape, 1) < half
    firsts = jnp.where(upper, low, pltpu.roll(high, half, 1))
    return firsts, jnp.where(upper, pltpu.roll(low, half, 1), high)


def product_kernel(incoming, devices, x, out):
    columns = x.shape[1]
    row_count = columns // devices
    per_device = x.shape[0] // (2 * columns)
    tiles = x[...].astype(F32).reshape(devices // 2, 2, per_device, 2 * row_count, columns)
    products = []
    for channel in range(per_device):
        sides = apart(tiles[:, 0, channel], tiles[:, 1, channel], row_count)
        left, right = (side.reshape(columns, columns).astype(BF16) for side in sides)
        products.append(
            lax.dot_general(
                left, right, ON_SUBLANES if incoming else ON_LANES, preferred_element_type=F32
            ).reshape(devices // 2, 2 * row_count, columns)
        )
    if per_device == 1:
        out[...] = products[0].reshape(columns, columns).astype(BF16)
        return
    even, odd = [], []
    for channel in range(0, per_device, 2):
        low, high = apart(products[channel], products[channel + 1], row_count)
        even.append(low)
        odd.append(high)
    merged = jnp.stack([jnp.stack(even, axis=1), jnp.stack(odd, axis=1)], axis=1)
    out[...] = merged.reshape(out.shape).astype(BF16)


def finish(y32, first, lanes, columns, gain, bias, weight):
    row_count = y32.shape[1] // gain.shape[0]
    normed = []
    for at in range(first, first + lanes, LANES):
        row, column = divmod(at, columns)
        rows = pl.ds(row, gain.shape[0], stride=row_count)
        normed.append(normalize(y32[column // LANES, rows, :], gain, bias))
    return jnp.dot(weight, jnp.concatenate(normed, axis=1), preferred_element_type=F32)


def middle_kernel(
    y, state, gating, mask, turned, weight_o, left, right, gate,
    out, state_out, gating_out, y32, e32,
):
    row_count, columns = mask.shape
    gain_o, bias_o = spread(turned[:, 0:1]), spread(turned[:, 2:3])
    gain, bias = spread(turned[:, 5:6]), spread(turned[:, 7:8])
    weight = jnp.transpose(weight_o[0] * 0.5)
    weights = turn_all(left[1], right[1], gate[1])
    widen(y, y32)
    for at in range(0, row_count * columns, 2 * LANES):
        lanes = slice(at, at + 2 * LANES)
        update = finish(y32, at, 2 * LANES, columns, gain_o, bias_o, weight)
        stored = (state[:, lanes] + gating[:, lanes] * update).astype(BF16)
        state_out[:, lanes] = stored
        values = stored.astype(F32)
        normed = [normalize(values[:, q : q + LANES], gain, bias) for q in (0, LANES)]
        project(jnp.concatenate(normed, axis=1), weights, at, mask, e32, gating_out)
    pack(e32, out)


def end_kernel(y, state, gating, turned, weight_o, out, y32):
    row_count, columns, channels = out.shape
    one = unit(1.0)
    gain_o, bias_o = spread(turned[:, 1:2]), spread(turned[:, 3:4])
    weight = jnp.transpose(weight_o[1] * 0.5)
    widen(y, y32)
    update = finish(y32, 0, row_count * columns, columns, gain_o, bias_o, weight)
    stored = (state[...].astype(F32) + gating[...] * update).astype(BF16)
    for row in range(row_count):
        lanes = slice(row * columns, (row + 1) * columns)
        out[row] = turn(one, stored[:, lanes])


def call(kernel, shapes, scratch, semaphores=0, far_in=False):
    near = pl.BlockSpec(memory_space=pltpu.VMEM)
    far = pl.BlockSpec(memory_space=pltpu.HBM)

    def run(*operands):
        if far_in:
            operands = [pltpu.with_memory_space_constraint(o, pltpu.HBM) for o in operands]
        return pl.pallas_call(
            kernel,
            out_shape=[jax.ShapeDtypeStruct(*s) for s in shapes],
            in_specs=[far if far_in else near] * len(operands),
            out_specs=[near] * len(shapes),
            scratch_shapes=[pltpu.VMEM(*s) for s in scratch]
            + [pltpu.SemaphoreType.DMA((semaphores,))] * (semaphores > 0),
            compiler_params=pltpu.CompilerParams(vmem_limit_bytes=16 << 20),
        )(*operands)

    return run


def exchange(rows):
    devices = lax.axis_size(AXES[0]) * lax.axis_size(AXES[1])
    count, columns = rows.shape
    moved = lax.all_to_all(
        rows.reshape(devices, count // devices, columns),
        AXES,
        split_axis=0,
        concat_axis=0,
        tiled=True,
    )
    return moved.reshape(count, columns)


def shards(
    pair_repr,
    pair_mask,
    chain_index,
    entity_embed,
    input_gain,
    input_bias,
    left_weight,
    right_weight,
    gate_weight,
    output_gain,
    output_bias,
    output_weight,
):
    row_count, columns, channels = pair_repr.shape
    hidden = output_weight.shape[1]
    devices = lax.axis_size(AXES[0]) * lax.axis_size(AXES[1])
    positions = row_count * columns
    edge = (hidden * 2 * row_count, columns)
    prod = (hidden * row_count, columns)
    wide = (channels, positions)

    def tall(shape):
        return ((shape[1] // LANES, shape[0], LANES), F32)

    columnar = ((channels, 8), F32)
    weights = [left_weight.shape[1:], right_weight.shape[1:], gate_weight.shape[1:]]

    sent, state, gating, mask, turned = call(
        start_kernel,
        [(edge, BF16), (wide, F32), (wide, F32), (pair_mask.shape, F32), columnar],
        [(pair_repr.shape, BF16), (pair_mask.shape, jnp.int32), ((1, columns), jnp.int32)]
        + [((2, channels), F32)] * 5
        + [(shape, BF16) for shape in weights]
        + [tall(edge), ((8, channels), F32)],
        semaphores=11,
        far_in=True,
    )(
        pair_repr, pair_mask, chain_index.reshape(1, -1), entity_embed, input_gain, input_bias,
        output_gain, output_bias, left_weight, right_weight, gate_weight,
    )

    def product(rows, incoming):
        return call(
            functools.partial(product_kernel, incoming, devices),
            [(prod, BF16)],
            [],
        )(rows)[0]

    back = exchange(product(exchange(sent), False))
    sent, state, gating = call(
        middle_kernel,
        [(edge, BF16), (wide, BF16), (wide, F32)],
        [tall(prod), tall(edge)],
    )(back, state, gating, mask, turned, output_weight, left_weight, right_weight, gate_weight)
    back = exchange(product(exchange(sent), True))
    return call(
        end_kernel,
        [(pair_repr.shape, BF16)],
        [tall(prod)],
    )(back, state, gating, turned, output_weight)[0]


def solution(mesh):
    rows = P(AXES, None)
    placed = (P(AXES, None, None), rows) + (P(),) * 10
    return jax.shard_map(
        shards, mesh=mesh, in_specs=placed, out_specs=P(AXES, None, None), check_vma=False
    )
```

```python
import functools

import jax
import jax.numpy as jnp
from jax import lax
from jax.experimental import pallas as pl
from jax.experimental.pallas import tpu as pltpu
from jax.sharding import PartitionSpec as P

AXES = ("grp", "blk")
F32, BF16 = jnp.float32, jnp.bfloat16
ON_SUBLANES = (((0,), (0,)), ((), ()))
ON_LANES = (((1,), (1,)), ((), ()))
LANES = 128


def unit(scale):
    down = lax.broadcasted_iota(jnp.int32, (LANES, LANES), 0)
    across = lax.broadcasted_iota(jnp.int32, (LANES, LANES), 1)
    return jnp.where(down == across, scale, 0.0).astype(BF16)


def turn(one, block):
    parts = [
        lax.dot_general(
            one, block[:, at : at + LANES], ON_LANES, preferred_element_type=F32
        ).astype(BF16)
        for at in range(0, block.shape[1], LANES)
    ]
    return jnp.concatenate(parts)


def turn_all(parts):
    scaled = [part if place in (1, 3) else part * 0.5 for place, part in enumerate(parts)]
    return jnp.transpose(jnp.concatenate(scaled, axis=1))


def halves(left, right, gate):
    hidden = left.shape[-1] // 2
    return [
        left[..., :hidden], left[..., hidden:], right[..., :hidden], right[..., hidden:], gate
    ]


def spread(column):
    return jnp.broadcast_to(column, (column.shape[0], LANES))


def normalize(values, gain, bias):
    average = jnp.mean(values, axis=0, keepdims=True)
    centered = values - average
    variance = jnp.mean(centered * centered, axis=0, keepdims=True)
    return (centered * lax.rsqrt(variance + 1e-05) * gain + bias).astype(BF16)


def put(ref, first, count, stride, values):
    for part in range(ref.shape[0]):
        at = part * LANES
        ref[part, pl.ds(first, count, stride=stride), :] = values[:, at : at + LANES]


def take(ref, first, count, stride):
    rows = pl.ds(first, count, stride=stride)
    return jnp.concatenate([ref[part, rows, :] for part in range(ref.shape[0])], axis=1)


def widen(source, ref):
    for part in range(ref.shape[0]):
        ref[part] = source[:, part * LANES : (part + 1) * LANES].astype(F32)


def pack(ref, out):
    for part in range(ref.shape[0]):
        out[:, part * LANES : (part + 1) * LANES] = ref[part].astype(BF16)


def project(normed, weights, first, mask, e32, gating):
    row_count, columns = mask.shape
    hidden = e32.shape[1] // (2 * row_count)
    projected = jnp.dot(weights, normed, preferred_element_type=F32)
    for at in range(0, normed.shape[1], LANES):
        row, column = divmod(first + at, columns)
        block = projected[:, at : at + LANES]
        kept = mask[row : row + 1, column : column + LANES]
        for side in range(2):
            low = 2 * hidden * side
            values = block[low + hidden : low + 2 * hidden] * kept
            values = (jnp.tanh(block[low : low + hidden]) + 1.0) * values
            rows = pl.ds(side * row_count + row, hidden, stride=2 * row_count)
            e32[column // LANES, rows, :] = values
        gating[:, first + at : first + at + LANES] = jnp.tanh(block[4 * hidden :]) + 1.0


def start_kernel(
    pair_h, mask_h, chain_h, embed_h, gain_h, bias_h, gain_oh, bias_oh, left_h, right_h, gate_h,
    out, state, gating, mask_out, columns_out,
    pair, mask, chain, small, weights, e32, rows, arrived,
):
    row_count, columns, channels = pair.shape
    moves = [(pair_h, pair, 0)]
    smalls = (embed_h, gain_h, bias_h, gain_oh, bias_oh)
    moves += [(source, small.at[place], 1) for place, source in enumerate(smalls)]
    moves += [(chain_h, chain, 2)]
    hidden = weights.shape[2]
    for place, source in enumerate((left_h, left_h, right_h, right_h, gate_h)):
        lanes = pl.ds(place % 2 * hidden, hidden)
        moves += [(source.at[0, :, lanes], weights.at[place], 3)]
    moves += [(mask_h, mask, 4)]
    for source, target, which in moves:
        pltpu.make_async_copy(source, target, arrived.at[which]).start()
    first = lax.axis_index(AXES) * row_count
    one = unit(1.0)

    def wait(whole, which):
        pltpu.make_async_copy(whole, whole, arrived.at[which]).wait()

    wait(small, 1)
    wait(chain, 2)
    wait(pair, 0)
    for place in range(4):
        rows[2 * place : 2 * place + 2, :] = small[(3, 4, 1, 2)[place]]
    turned = jnp.transpose(rows[...])
    columns_out[...] = turned
    gain_c, bias_c = spread(turned[:, 4:5]), spread(turned[:, 6:7])
    rows[0:2, :] = small[0]
    turned = jnp.transpose(rows[...])
    other, same = spread(turned[:, 0:1]), spread(turned[:, 1:2])
    chains = jnp.broadcast_to(chain[...].astype(F32), (row_count, chain.shape[1]))
    place = lax.broadcasted_iota(jnp.int32, chains.shape, 1)
    mine = first + lax.broadcasted_iota(jnp.int32, chains.shape, 0)
    own = jnp.sum(jnp.where(place == mine, chains, 0.0), axis=1, keepdims=True)
    alike = jnp.where(chains == own, 1.0, 0.0)
    normed = []
    for begin in range(0, row_count * columns, LANES):
        row, column = divmod(begin, columns)
        values = lax.dot_general(
            one, pair[row, column : column + LANES, :], ON_LANES, preferred_element_type=F32
        )
        hit = jnp.broadcast_to(alike[row : row + 1, column : column + LANES], values.shape)
        values = values + jnp.where(hit > 0.5, same, other)
        state[:, begin : begin + LANES] = values
        normed.append(normalize(values, gain_c, bias_c))
    wait(weights, 3)
    wait(mask, 4)
    mask_out[...] = mask[...].astype(F32) * 0.5
    turned = turn_all([weights[place] for place in range(weights.shape[0])])
    for place in range(0, len(normed), 2):
        pair_of = jnp.concatenate(normed[place : place + 2], axis=1)
        project(pair_of, turned, place * LANES, mask_out, e32, gating)
    pack(e32, out)


def apart(low, high, half):
    upper = lax.broadcasted_iota(jnp.int32, low.shape, 1) < half
    firsts = jnp.where(upper, low, pltpu.roll(high, half, 1))
    return firsts, jnp.where(upper, pltpu.roll(low, half, 1), high)


def product_kernel(incoming, devices, x, out):
    columns = x.shape[1]
    row_count = columns // devices
    per_device = x.shape[0] // (2 * columns)
    tiles = x[...].astype(F32).reshape(devices // 2, 2, per_device, 2 * row_count, columns)
    products = []
    for channel in range(per_device):
        sides = apart(tiles[:, 0, channel], tiles[:, 1, channel], row_count)
        left, right = (side.reshape(columns, columns).astype(BF16) for side in sides)
        products.append(
            lax.dot_general(
                left, right, ON_SUBLANES if incoming else ON_LANES, preferred_element_type=F32
            ).reshape(devices // 2, 2 * row_count, columns)
        )
    if per_device == 1:
        out[...] = products[0].reshape(columns, columns).astype(BF16)
        return
    even, odd = [], []
    for channel in range(0, per_device, 2):
        low, high = apart(products[channel], products[channel + 1], row_count)
        even.append(low)
        odd.append(high)
    merged = jnp.stack([jnp.stack(even, axis=1), jnp.stack(odd, axis=1)], axis=1)
    out[...] = merged.reshape(out.shape).astype(BF16)


def finish(y32, first, lanes, columns, gain, bias, weight):
    row_count = y32.shape[1] // gain.shape[0]
    normed = []
    for at in range(first, first + lanes, LANES):
        row, column = divmod(at, columns)
        rows = pl.ds(row, gain.shape[0], stride=row_count)
        normed.append(normalize(y32[column // LANES, rows, :], gain, bias))
    return jnp.dot(weight, jnp.concatenate(normed, axis=1), preferred_element_type=F32)


def middle_kernel(
    y, state, gating, mask, turned, weight_o, left, right, gate,
    out, state_out, gating_out, y32, e32,
):
    row_count, columns = mask.shape
    gain_o, bias_o = spread(turned[:, 0:1]), spread(turned[:, 2:3])
    gain, bias = spread(turned[:, 5:6]), spread(turned[:, 7:8])
    weight = jnp.transpose(weight_o[0] * 0.5)
    weights = turn_all(halves(left[1], right[1], gate[1]))
    widen(y, y32)
    for at in range(0, row_count * columns, 2 * LANES):
        lanes = slice(at, at + 2 * LANES)
        update = finish(y32, at, 2 * LANES, columns, gain_o, bias_o, weight)
        stored = (state[:, lanes] + gating[:, lanes] * update).astype(BF16)
        state_out[:, lanes] = stored
        values = stored.astype(F32)
        normed = [normalize(values[:, q : q + LANES], gain, bias) for q in (0, LANES)]
        project(jnp.concatenate(normed, axis=1), weights, at, mask, e32, gating_out)
    pack(e32, out)


def end_kernel(y, state, gating, turned, weight_o, out, y32):
    row_count, columns, channels = out.shape
    one = unit(1.0)
    gain_o, bias_o = spread(turned[:, 1:2]), spread(turned[:, 3:4])
    weight = jnp.transpose(weight_o[1] * 0.5)
    widen(y, y32)
    update = finish(y32, 0, row_count * columns, columns, gain_o, bias_o, weight)
    stored = (state[...].astype(F32) + gating[...] * update).astype(BF16)
    for row in range(row_count):
        lanes = slice(row * columns, (row + 1) * columns)
        out[row] = turn(one, stored[:, lanes])


def call(kernel, shapes, scratch, semaphores=0, far_in=False):
    near = pl.BlockSpec(memory_space=pltpu.VMEM)
    far = pl.BlockSpec(memory_space=pltpu.HBM)

    def run(*operands):
        if far_in:
            operands = [pltpu.with_memory_space_constraint(o, pltpu.HBM) for o in operands]
        return pl.pallas_call(
            kernel,
            out_shape=[jax.ShapeDtypeStruct(*s) for s in shapes],
            in_specs=[far if far_in else near] * len(operands),
            out_specs=[near] * len(shapes),
            scratch_shapes=[pltpu.VMEM(*s) for s in scratch]
            + [pltpu.SemaphoreType.DMA((semaphores,))] * (semaphores > 0),
            compiler_params=pltpu.CompilerParams(vmem_limit_bytes=16 << 20),
        )(*operands)

    return run


def exchange(rows):
    devices = lax.axis_size(AXES[0]) * lax.axis_size(AXES[1])
    count, columns = rows.shape
    moved = lax.all_to_all(
        rows.reshape(devices, count // devices, columns),
        AXES,
        split_axis=0,
        concat_axis=0,
        tiled=True,
    )
    return moved.reshape(count, columns)


def shards(
    pair_repr,
    pair_mask,
    chain_index,
    entity_embed,
    input_gain,
    input_bias,
    left_weight,
    right_weight,
    gate_weight,
    output_gain,
    output_bias,
    output_weight,
):
    row_count, columns, channels = pair_repr.shape
    hidden = output_weight.shape[1]
    devices = lax.axis_size(AXES[0]) * lax.axis_size(AXES[1])
    positions = row_count * columns
    edge = (hidden * 2 * row_count, columns)
    prod = (hidden * row_count, columns)
    wide = (channels, positions)

    def tall(shape):
        return ((shape[1] // LANES, shape[0], LANES), F32)

    columnar = ((channels, 8), F32)

    sent, state, gating, mask, turned = call(
        start_kernel,
        [(edge, BF16), (wide, F32), (wide, F32), (pair_mask.shape, F32), columnar],
        [(pair_repr.shape, BF16), (pair_mask.shape, jnp.int32), ((1, columns), jnp.int32)]
        + [((5, 2, channels), F32), ((5, channels, hidden), BF16), tall(edge), ((8, channels), F32)],
        semaphores=5,
        far_in=True,
    )(
        pair_repr, pair_mask, chain_index.reshape(1, -1), entity_embed, input_gain, input_bias,
        output_gain, output_bias, left_weight, right_weight, gate_weight,
    )

    def product(rows, incoming):
        return call(
            functools.partial(product_kernel, incoming, devices),
            [(prod, BF16)],
            [],
        )(rows)[0]

    back = exchange(product(exchange(sent), False))
    sent, state, gating = call(
        middle_kernel,
        [(edge, BF16), (wide, BF16), (wide, F32)],
        [tall(prod), tall(edge)],
    )(back, state, gating, mask, turned, output_weight, left_weight, right_weight, gate_weight)
    back = exchange(product(exchange(sent), True))
    return call(
        end_kernel,
        [(pair_repr.shape, BF16)],
        [tall(prod)],
    )(back, state, gating, turned, output_weight)[0]


def solution(mesh):
    rows = P(AXES, None)
    placed = (P(AXES, None, None), rows) + (P(),) * 10
    return jax.shard_map(
        shards, mesh=mesh, in_specs=placed, out_specs=P(AXES, None, None), check_vma=False
    )
```

```python
import functools

import jax
import jax.numpy as jnp
from jax import lax
from jax.experimental import pallas as pl
from jax.experimental.pallas import tpu as pltpu
from jax.sharding import PartitionSpec as P

AXES = ("grp", "blk")
F32, BF16 = jnp.float32, jnp.bfloat16
ON_SUBLANES = (((0,), (0,)), ((), ()))
ON_LANES = (((1,), (1,)), ((), ()))
LANES = 128


def unit(scale):
    down = lax.broadcasted_iota(jnp.int32, (LANES, LANES), 0)
    across = lax.broadcasted_iota(jnp.int32, (LANES, LANES), 1)
    return jnp.where(down == across, scale, 0.0).astype(BF16)


def turn(one, block):
    parts = [
        lax.dot_general(
            one, block[:, at : at + LANES], ON_LANES, preferred_element_type=F32
        ).astype(BF16)
        for at in range(0, block.shape[1], LANES)
    ]
    return jnp.concatenate(parts)


def turn_all(parts):
    scaled = [part if place in (1, 3) else part * 0.5 for place, part in enumerate(parts)]
    return jnp.transpose(jnp.concatenate(scaled, axis=1))


def halves(left, right, gate):
    hidden = left.shape[-1] // 2
    return [
        left[..., :hidden], left[..., hidden:], right[..., :hidden], right[..., hidden:], gate
    ]


def spread(column):
    return jnp.broadcast_to(column, (column.shape[0], LANES))


def normalize(values, gain, bias):
    average = jnp.mean(values, axis=0, keepdims=True)
    centered = values - average
    variance = jnp.mean(centered * centered, axis=0, keepdims=True)
    return (centered * lax.rsqrt(variance + 1e-05) * gain + bias).astype(BF16)


def put(ref, first, count, stride, values):
    for part in range(ref.shape[0]):
        at = part * LANES
        ref[part, pl.ds(first, count, stride=stride), :] = values[:, at : at + LANES]


def take(ref, first, count, stride):
    rows = pl.ds(first, count, stride=stride)
    return jnp.concatenate([ref[part, rows, :] for part in range(ref.shape[0])], axis=1)


def widen(source, ref):
    for part in range(ref.shape[0]):
        ref[part] = source[:, part * LANES : (part + 1) * LANES].astype(F32)


def pack(ref, out):
    for part in range(ref.shape[0]):
        out[:, part * LANES : (part + 1) * LANES] = ref[part].astype(BF16)


def project(normed, weights, first, mask, e32, gating):
    row_count, columns = mask.shape
    hidden = e32.shape[1] // (2 * row_count)
    projected = jnp.dot(weights, normed, preferred_element_type=F32)
    for at in range(0, normed.shape[1], LANES):
        row, column = divmod(first + at, columns)
        block = projected[:, at : at + LANES]
        kept = mask[row : row + 1, column : column + LANES]
        for side in range(2):
            low = 2 * hidden * side
            values = block[low + hidden : low + 2 * hidden] * kept
            values = (jnp.tanh(block[low : low + hidden]) + 1.0) * values
            rows = pl.ds(side * row_count + row, hidden, stride=2 * row_count)
            e32[column // LANES, rows, :] = values
        gating[:, first + at : first + at + LANES] = jnp.tanh(block[4 * hidden :]) + 1.0


def start_kernel(
    pair_h, mask_h, chain_h, embed_h, gain_h, bias_h, gain_oh, bias_oh, left_h, right_h, gate_h,
    out, state, gating, mask_out, columns_out,
    pair, mask, chain, small, weights, e32, rows, arrived,
):
    row_count, columns, channels = pair.shape
    moves = [(pair_h.at[row], pair.at[row], 0) for row in range(row_count)]
    smalls = (embed_h, gain_h, bias_h, gain_oh, bias_oh)
    moves += [(source, small.at[place], 1) for place, source in enumerate(smalls)]
    moves += [(chain_h, chain, 2)]
    hidden = weights.shape[2]
    for place, source in enumerate((left_h, left_h, right_h, right_h, gate_h)):
        lanes = pl.ds(place % 2 * hidden, hidden)
        moves += [(source.at[0, :, lanes], weights.at[place], 3)]
    moves += [(mask_h, mask, 4)]
    for source, target, which in moves:
        pltpu.make_async_copy(source, target, arrived.at[which]).start()
    first = lax.axis_index(AXES) * row_count
    one = unit(1.0)

    def wait(whole, which):
        pltpu.make_async_copy(whole, whole, arrived.at[which]).wait()

    wait(small, 1)
    wait(chain, 2)
    wait(pair, 0)
    for place in range(4):
        rows[2 * place : 2 * place + 2, :] = small[(3, 4, 1, 2)[place]]
    turned = jnp.transpose(rows[...])
    columns_out[...] = turned
    gain_c, bias_c = spread(turned[:, 4:5]), spread(turned[:, 6:7])
    rows[0:2, :] = small[0]
    turned = jnp.transpose(rows[...])
    other, same = spread(turned[:, 0:1]), spread(turned[:, 1:2])
    chains = jnp.broadcast_to(chain[...].astype(F32), (row_count, chain.shape[1]))
    place = lax.broadcasted_iota(jnp.int32, chains.shape, 1)
    mine = first + lax.broadcasted_iota(jnp.int32, chains.shape, 0)
    own = jnp.sum(jnp.where(place == mine, chains, 0.0), axis=1, keepdims=True)
    alike = jnp.where(chains == own, 1.0, 0.0)
    normed = []
    for begin in range(0, row_count * columns, LANES):
        row, column = divmod(begin, columns)
        values = lax.dot_general(
            one, pair[row, column : column + LANES, :], ON_LANES, preferred_element_type=F32
        )
        hit = jnp.broadcast_to(alike[row : row + 1, column : column + LANES], values.shape)
        values = values + jnp.where(hit > 0.5, same, other)
        state[:, begin : begin + LANES] = values
        normed.append(normalize(values, gain_c, bias_c))
    wait(weights, 3)
    wait(mask, 4)
    mask_out[...] = mask[...].astype(F32) * 0.5
    turned = turn_all([weights[place] for place in range(weights.shape[0])])
    for place in range(0, len(normed), 2):
        pair_of = jnp.concatenate(normed[place : place + 2], axis=1)
        project(pair_of, turned, place * LANES, mask_out, e32, gating)
    pack(e32, out)


def apart(low, high, half):
    upper = lax.broadcasted_iota(jnp.int32, low.shape, 1) < half
    firsts = jnp.where(upper, low, pltpu.roll(high, half, 1))
    return firsts, jnp.where(upper, pltpu.roll(low, half, 1), high)


def product_kernel(incoming, devices, x, out):
    columns = x.shape[1]
    row_count = columns // devices
    per_device = x.shape[0] // (2 * columns)
    tiles = x[...].astype(F32).reshape(devices // 2, 2, per_device, 2 * row_count, columns)
    products = []
    for channel in range(per_device):
        sides = apart(tiles[:, 0, channel], tiles[:, 1, channel], row_count)
        left, right = (side.reshape(columns, columns).astype(BF16) for side in sides)
        products.append(
            lax.dot_general(
                left, right, ON_SUBLANES if incoming else ON_LANES, preferred_element_type=F32
            ).reshape(devices // 2, 2 * row_count, columns)
        )
    if per_device == 1:
        out[...] = products[0].reshape(columns, columns).astype(BF16)
        return
    even, odd = [], []
    for channel in range(0, per_device, 2):
        low, high = apart(products[channel], products[channel + 1], row_count)
        even.append(low)
        odd.append(high)
    merged = jnp.stack([jnp.stack(even, axis=1), jnp.stack(odd, axis=1)], axis=1)
    out[...] = merged.reshape(out.shape).astype(BF16)


def finish(y32, first, lanes, columns, gain, bias, weight):
    row_count = y32.shape[1] // gain.shape[0]
    normed = []
    for at in range(first, first + lanes, LANES):
        row, column = divmod(at, columns)
        rows = pl.ds(row, gain.shape[0], stride=row_count)
        normed.append(normalize(y32[column // LANES, rows, :], gain, bias))
    return jnp.dot(weight, jnp.concatenate(normed, axis=1), preferred_element_type=F32)


def middle_kernel(
    y, state, gating, mask, turned, weight_o, left, right, gate,
    out, state_out, gating_out, y32, e32,
):
    row_count, columns = mask.shape
    gain_o, bias_o = spread(turned[:, 0:1]), spread(turned[:, 2:3])
    gain, bias = spread(turned[:, 5:6]), spread(turned[:, 7:8])
    weight = jnp.transpose(weight_o[0] * 0.5)
    weights = turn_all(halves(left[1], right[1], gate[1]))
    widen(y, y32)
    for at in range(0, row_count * columns, 2 * LANES):
        lanes = slice(at, at + 2 * LANES)
        update = finish(y32, at, 2 * LANES, columns, gain_o, bias_o, weight)
        stored = (state[:, lanes] + gating[:, lanes] * update).astype(BF16)
        state_out[:, lanes] = stored
        values = stored.astype(F32)
        normed = [normalize(values[:, q : q + LANES], gain, bias) for q in (0, LANES)]
        project(jnp.concatenate(normed, axis=1), weights, at, mask, e32, gating_out)
    pack(e32, out)


def end_kernel(y, state, gating, turned, weight_o, out, y32):
    row_count, columns, channels = out.shape
    one = unit(1.0)
    gain_o, bias_o = spread(turned[:, 1:2]), spread(turned[:, 3:4])
    weight = jnp.transpose(weight_o[1] * 0.5)
    widen(y, y32)
    update = finish(y32, 0, row_count * columns, columns, gain_o, bias_o, weight)
    stored = (state[...].astype(F32) + gating[...] * update).astype(BF16)
    for row in range(row_count):
        lanes = slice(row * columns, (row + 1) * columns)
        out[row] = turn(one, stored[:, lanes])


def call(kernel, shapes, scratch, semaphores=0, far_in=False):
    near = pl.BlockSpec(memory_space=pltpu.VMEM)
    far = pl.BlockSpec(memory_space=pltpu.HBM)

    def run(*operands):
        if far_in:
            operands = [pltpu.with_memory_space_constraint(o, pltpu.HBM) for o in operands]
        return pl.pallas_call(
            kernel,
            out_shape=[jax.ShapeDtypeStruct(*s) for s in shapes],
            in_specs=[far if far_in else near] * len(operands),
            out_specs=[near] * len(shapes),
            scratch_shapes=[pltpu.VMEM(*s) for s in scratch]
            + [pltpu.SemaphoreType.DMA((semaphores,))] * (semaphores > 0),
            compiler_params=pltpu.CompilerParams(vmem_limit_bytes=16 << 20),
        )(*operands)

    return run


def exchange(rows):
    devices = lax.axis_size(AXES[0]) * lax.axis_size(AXES[1])
    count, columns = rows.shape
    moved = lax.all_to_all(
        rows.reshape(devices, count // devices, columns),
        AXES,
        split_axis=0,
        concat_axis=0,
        tiled=True,
    )
    return moved.reshape(count, columns)


def shards(
    pair_repr,
    pair_mask,
    chain_index,
    entity_embed,
    input_gain,
    input_bias,
    left_weight,
    right_weight,
    gate_weight,
    output_gain,
    output_bias,
    output_weight,
):
    row_count, columns, channels = pair_repr.shape
    hidden = output_weight.shape[1]
    devices = lax.axis_size(AXES[0]) * lax.axis_size(AXES[1])
    positions = row_count * columns
    edge = (hidden * 2 * row_count, columns)
    prod = (hidden * row_count, columns)
    wide = (channels, positions)

    def tall(shape):
        return ((shape[1] // LANES, shape[0], LANES), F32)

    columnar = ((channels, 8), F32)

    sent, state, gating, mask, turned = call(
        start_kernel,
        [(edge, BF16), (wide, F32), (wide, F32), (pair_mask.shape, F32), columnar],
        [(pair_repr.shape, BF16), (pair_mask.shape, jnp.int32), ((1, columns), jnp.int32)]
        + [((5, 2, channels), F32), ((5, channels, hidden), BF16), tall(edge), ((8, channels), F32)],
        semaphores=5,
        far_in=True,
    )(
        pair_repr, pair_mask, chain_index.reshape(1, -1), entity_embed, input_gain, input_bias,
        output_gain, output_bias, left_weight, right_weight, gate_weight,
    )

    def product(rows, incoming):
        return call(
            functools.partial(product_kernel, incoming, devices),
            [(prod, BF16)],
            [],
        )(rows)[0]

    back = exchange(product(exchange(sent), False))
    sent, state, gating = call(
        middle_kernel,
        [(edge, BF16), (wide, BF16), (wide, F32)],
        [tall(prod), tall(edge)],
    )(back, state, gating, mask, turned, output_weight, left_weight, right_weight, gate_weight)
    back = exchange(product(exchange(sent), True))
    return call(
        end_kernel,
        [(pair_repr.shape, BF16)],
        [tall(prod)],
    )(back, state, gating, turned, output_weight)[0]


def solution(mesh):
    rows = P(AXES, None)
    placed = (P(AXES, None, None), rows) + (P(),) * 10
    return jax.shard_map(
        shards, mesh=mesh, in_specs=placed, out_specs=P(AXES, None, None), check_vma=False
    )
```

```python
import functools

import jax
import jax.numpy as jnp
from jax import lax
from jax.experimental import pallas as pl
from jax.experimental.pallas import tpu as pltpu
from jax.sharding import PartitionSpec as P

AXES = ("grp", "blk")
F32, BF16 = jnp.float32, jnp.bfloat16
ON_SUBLANES = (((0,), (0,)), ((), ()))
ON_LANES = (((1,), (1,)), ((), ()))
LANES = 128


def unit(scale):
    down = lax.broadcasted_iota(jnp.int32, (LANES, LANES), 0)
    across = lax.broadcasted_iota(jnp.int32, (LANES, LANES), 1)
    return jnp.where(down == across, scale, 0.0).astype(BF16)


def turn(one, block):
    parts = [
        lax.dot_general(
            one, block[:, at : at + LANES], ON_LANES, preferred_element_type=F32
        ).astype(BF16)
        for at in range(0, block.shape[1], LANES)
    ]
    return jnp.concatenate(parts)


def turn_all(parts):
    scaled = [part if place in (1, 3) else part * 0.5 for place, part in enumerate(parts)]
    return jnp.transpose(jnp.concatenate(scaled, axis=1))


def halves(left, right, gate):
    hidden = left.shape[-1] // 2
    return [
        left[..., :hidden], left[..., hidden:], right[..., :hidden], right[..., hidden:], gate
    ]


def spread(column):
    return jnp.broadcast_to(column, (column.shape[0], LANES))


def normalize(values, gain, bias):
    average = jnp.mean(values, axis=0, keepdims=True)
    centered = values - average
    variance = jnp.mean(centered * centered, axis=0, keepdims=True)
    return (centered * lax.rsqrt(variance + 1e-05) * gain + bias).astype(BF16)


def put(ref, first, count, stride, values):
    for part in range(ref.shape[0]):
        at = part * LANES
        ref[part, pl.ds(first, count, stride=stride), :] = values[:, at : at + LANES]


def take(ref, first, count, stride):
    rows = pl.ds(first, count, stride=stride)
    return jnp.concatenate([ref[part, rows, :] for part in range(ref.shape[0])], axis=1)


def widen(source, ref):
    for part in range(ref.shape[0]):
        ref[part] = source[:, part * LANES : (part + 1) * LANES].astype(F32)


def pack(ref, out):
    for part in range(ref.shape[0]):
        out[:, part * LANES : (part + 1) * LANES] = ref[part].astype(BF16)


def project(normed, weights, first, mask, e32, gating):
    row_count, columns = mask.shape
    hidden = e32.shape[1] // (2 * row_count)
    projected = jnp.dot(weights, normed, preferred_element_type=F32)
    for at in range(0, normed.shape[1], LANES):
        row, column = divmod(first + at, columns)
        block = projected[:, at : at + LANES]
        kept = mask[row : row + 1, column : column + LANES]
        for side in range(2):
            low = 2 * hidden * side
            values = block[low + hidden : low + 2 * hidden] * kept
            values = (jnp.tanh(block[low : low + hidden]) + 1.0) * values
            rows = pl.ds(side * row_count + row, hidden, stride=2 * row_count)
            e32[column // LANES, rows, :] = values
        gating[:, first + at : first + at + LANES] = jnp.tanh(block[4 * hidden :]) + 1.0


def start_kernel(
    pair_h, mask_h, chain_h, embed_h, gain_h, bias_h, gain_oh, bias_oh, left_h, right_h, gate_h,
    out, state, gating, mask_out, columns_out,
    pair, mask, chain, small, weights, e32, rows, arrived,
):
    row_count, columns, channels = pair.shape
    moves = [(pair_h.at[row], pair.at[row], 0) for row in range(row_count)]
    smalls = (embed_h, gain_h, bias_h, gain_oh, bias_oh)
    moves += [(source, small.at[place], 1) for place, source in enumerate(smalls)]
    moves += [(chain_h, chain, 2)]
    hidden = weights.shape[2]
    for place, source in enumerate((left_h, left_h, right_h, right_h, gate_h)):
        lanes = pl.ds(place % 2 * hidden, hidden)
        moves += [(source.at[0, :, lanes], weights.at[place], 3)]
    moves += [(mask_h, mask, 4)]
    for source, target, which in moves:
        pltpu.make_async_copy(source, target, arrived.at[which]).start()
    first = lax.axis_index(AXES) * row_count
    one = unit(1.0)

    def wait(whole, which):
        pltpu.make_async_copy(whole, whole, arrived.at[which]).wait()

    wait(small, 1)
    wait(chain, 2)
    wait(pair, 0)
    for place in range(4):
        rows[2 * place : 2 * place + 2, :] = small[(3, 4, 1, 2)[place]]
    turned = jnp.transpose(rows[...])
    columns_out[...] = turned
    gain_c, bias_c = spread(turned[:, 4:5]), spread(turned[:, 6:7])
    rows[0:2, :] = small[0]
    turned = jnp.transpose(rows[...])
    other, same = spread(turned[:, 0:1]), spread(turned[:, 1:2])
    chains = jnp.broadcast_to(chain[...].astype(F32), (row_count, chain.shape[1]))
    place = lax.broadcasted_iota(jnp.int32, chains.shape, 1)
    mine = first + lax.broadcasted_iota(jnp.int32, chains.shape, 0)
    own = jnp.sum(jnp.where(place == mine, chains, 0.0), axis=1, keepdims=True)
    alike = jnp.where(chains == own, 1.0, 0.0)
    normed = []
    for begin in range(0, row_count * columns, LANES):
        row, column = divmod(begin, columns)
        values = lax.dot_general(
            one, pair[row, column : column + LANES, :], ON_LANES, preferred_element_type=F32
        )
        hit = jnp.broadcast_to(alike[row : row + 1, column : column + LANES], values.shape)
        values = values + jnp.where(hit > 0.5, same, other)
        state[:, begin : begin + LANES] = values
        normed.append(normalize(values, gain_c, bias_c))
    wait(weights, 3)
    wait(mask, 4)
    mask_out[...] = mask[...].astype(F32) * 0.5
    turned = turn_all([weights[place] for place in range(weights.shape[0])])
    for place in range(0, len(normed), 2):
        pair_of = jnp.concatenate(normed[place : place + 2], axis=1)
        project(pair_of, turned, place * LANES, mask_out, e32, gating)
    pack(e32, out)


def apart(low, high, half):
    upper = lax.broadcasted_iota(jnp.int32, low.shape, 1) < half
    firsts = jnp.where(upper, low, pltpu.roll(high, half, 1))
    return firsts, jnp.where(upper, pltpu.roll(low, half, 1), high)


def product_kernel(incoming, devices, x, out):
    columns = x.shape[1]
    row_count = columns // devices
    per_device = x.shape[0] // (2 * columns)
    tiles = x[...].astype(F32).reshape(devices // 2, 2, per_device, 2 * row_count, columns)
    products = []
    for channel in range(per_device):
        sides = apart(tiles[:, 0, channel], tiles[:, 1, channel], row_count)
        left, right = (side.reshape(columns, columns).astype(BF16) for side in sides)
        products.append(
            lax.dot_general(
                left, right, ON_SUBLANES if incoming else ON_LANES, preferred_element_type=F32
            ).reshape(devices // 2, 2 * row_count, columns)
        )
    if per_device == 1:
        out[...] = products[0].reshape(columns, columns).astype(BF16)
        return
    even, odd = [], []
    for channel in range(0, per_device, 2):
        low, high = apart(products[channel], products[channel + 1], row_count)
        even.append(low)
        odd.append(high)
    merged = jnp.stack([jnp.stack(even, axis=1), jnp.stack(odd, axis=1)], axis=1)
    out[...] = merged.reshape(out.shape).astype(BF16)


def finish(y32, first, lanes, columns, gain, bias, weight):
    row_count = y32.shape[1] // gain.shape[0]
    normed = []
    for at in range(first, first + lanes, LANES):
        row, column = divmod(at, columns)
        rows = pl.ds(row, gain.shape[0], stride=row_count)
        normed.append(normalize(y32[column // LANES, rows, :], gain, bias))
    return jnp.dot(weight, jnp.concatenate(normed, axis=1), preferred_element_type=F32)


def middle_kernel(
    y, state, gating, mask, turned, weight_o, left, right, gate,
    out, state_out, gating_out, y32, e32,
):
    row_count, columns = mask.shape
    gain_o, bias_o = spread(turned[:, 0:1]), spread(turned[:, 2:3])
    gain, bias = spread(turned[:, 5:6]), spread(turned[:, 7:8])
    weight = jnp.transpose(weight_o[0] * 0.5)
    weights = turn_all(halves(left[1], right[1], gate[1]))
    widen(y, y32)
    for at in range(0, row_count * columns, 2 * LANES):
        lanes = slice(at, at + 2 * LANES)
        update = finish(y32, at, 2 * LANES, columns, gain_o, bias_o, weight)
        stored = (state[:, lanes] + gating[:, lanes] * update).astype(BF16)
        state_out[:, lanes] = stored
        values = stored.astype(F32)
        normed = [normalize(values[:, q : q + LANES], gain, bias) for q in (0, LANES)]
        project(jnp.concatenate(normed, axis=1), weights, at, mask, e32, gating_out)
    pack(e32, out)


def end_kernel(y, state, gating, turned, weight_o, out, y32):
    row_count, columns, channels = out.shape
    gain_o, bias_o = spread(turned[:, 1:2]), spread(turned[:, 3:4])
    weight = jnp.transpose(weight_o[1] * 0.5)
    widen(y, y32)
    update = finish(y32, 0, row_count * columns, columns, gain_o, bias_o, weight)
    stored = (state[...].astype(F32) + gating[...] * update).astype(BF16)
    for row in range(row_count):
        lanes = slice(row * columns, (row + 1) * columns)
        out[row] = jnp.transpose(stored[:, lanes])


def call(kernel, shapes, scratch, semaphores=0, far_in=False):
    near = pl.BlockSpec(memory_space=pltpu.VMEM)
    far = pl.BlockSpec(memory_space=pltpu.HBM)

    def run(*operands):
        if far_in:
            operands = [pltpu.with_memory_space_constraint(o, pltpu.HBM) for o in operands]
        return pl.pallas_call(
            kernel,
            out_shape=[jax.ShapeDtypeStruct(*s) for s in shapes],
            in_specs=[far if far_in else near] * len(operands),
            out_specs=[near] * len(shapes),
            scratch_shapes=[pltpu.VMEM(*s) for s in scratch]
            + [pltpu.SemaphoreType.DMA((semaphores,))] * (semaphores > 0),
            compiler_params=pltpu.CompilerParams(vmem_limit_bytes=16 << 20),
        )(*operands)

    return run


def exchange(rows):
    devices = lax.axis_size(AXES[0]) * lax.axis_size(AXES[1])
    count, columns = rows.shape
    moved = lax.all_to_all(
        rows.reshape(devices, count // devices, columns),
        AXES,
        split_axis=0,
        concat_axis=0,
        tiled=True,
    )
    return moved.reshape(count, columns)


def shards(
    pair_repr,
    pair_mask,
    chain_index,
    entity_embed,
    input_gain,
    input_bias,
    left_weight,
    right_weight,
    gate_weight,
    output_gain,
    output_bias,
    output_weight,
):
    row_count, columns, channels = pair_repr.shape
    hidden = output_weight.shape[1]
    devices = lax.axis_size(AXES[0]) * lax.axis_size(AXES[1])
    positions = row_count * columns
    edge = (hidden * 2 * row_count, columns)
    prod = (hidden * row_count, columns)
    wide = (channels, positions)

    def tall(shape):
        return ((shape[1] // LANES, shape[0], LANES), F32)

    columnar = ((channels, 8), F32)

    sent, state, gating, mask, turned = call(
        start_kernel,
        [(edge, BF16), (wide, F32), (wide, F32), (pair_mask.shape, F32), columnar],
        [(pair_repr.shape, BF16), (pair_mask.shape, jnp.int32), ((1, columns), jnp.int32)]
        + [((5, 2, channels), F32), ((5, channels, hidden), BF16), tall(edge), ((8, channels), F32)],
        semaphores=5,
        far_in=True,
    )(
        pair_repr, pair_mask, chain_index.reshape(1, -1), entity_embed, input_gain, input_bias,
        output_gain, output_bias, left_weight, right_weight, gate_weight,
    )

    def product(rows, incoming):
        return call(
            functools.partial(product_kernel, incoming, devices),
            [(prod, BF16)],
            [],
        )(rows)[0]

    back = exchange(product(exchange(sent), False))
    sent, state, gating = call(
        middle_kernel,
        [(edge, BF16), (wide, BF16), (wide, F32)],
        [tall(prod), tall(edge)],
    )(back, state, gating, mask, turned, output_weight, left_weight, right_weight, gate_weight)
    back = exchange(product(exchange(sent), True))
    return call(
        end_kernel,
        [(pair_repr.shape, BF16)],
        [tall(prod)],
    )(back, state, gating, turned, output_weight)[0]


def solution(mesh):
    rows = P(AXES, None)
    placed = (P(AXES, None, None), rows) + (P(),) * 10
    return jax.shard_map(
        shards, mesh=mesh, in_specs=placed, out_specs=P(AXES, None, None), check_vma=False
    )
```

```python
import functools

import jax
import jax.numpy as jnp
from jax import lax
from jax.experimental import pallas as pl
from jax.experimental.pallas import tpu as pltpu
from jax.sharding import PartitionSpec as P

AXES = ("grp", "blk")
F32, BF16 = jnp.float32, jnp.bfloat16
ON_SUBLANES = (((0,), (0,)), ((), ()))
ON_LANES = (((1,), (1,)), ((), ()))
LANES = 128


def unit(scale):
    down = lax.broadcasted_iota(jnp.int32, (LANES, LANES), 0)
    across = lax.broadcasted_iota(jnp.int32, (LANES, LANES), 1)
    return jnp.where(down == across, scale, 0.0).astype(BF16)


def turn(one, block):
    parts = [
        lax.dot_general(
            one, block[:, at : at + LANES], ON_LANES, preferred_element_type=F32
        ).astype(BF16)
        for at in range(0, block.shape[1], LANES)
    ]
    return jnp.concatenate(parts)


def turn_all(parts):
    scaled = [part if place in (1, 3) else part * 0.5 for place, part in enumerate(parts)]
    return jnp.transpose(jnp.concatenate(scaled, axis=1))


def halves(left, right, gate):
    hidden = left.shape[-1] // 2
    return [
        left[..., :hidden], left[..., hidden:], right[..., :hidden], right[..., hidden:], gate
    ]


def spread(column):
    return jnp.broadcast_to(column, (column.shape[0], LANES))


def normalize(values, gain, bias):
    average = jnp.mean(values, axis=0, keepdims=True)
    centered = values - average
    variance = jnp.mean(centered * centered, axis=0, keepdims=True)
    return (centered * lax.rsqrt(variance + 1e-05) * gain + bias).astype(BF16)


def put(ref, first, count, stride, values):
    for part in range(ref.shape[0]):
        at = part * LANES
        ref[part, pl.ds(first, count, stride=stride), :] = values[:, at : at + LANES]


def take(ref, first, count, stride):
    rows = pl.ds(first, count, stride=stride)
    return jnp.concatenate([ref[part, rows, :] for part in range(ref.shape[0])], axis=1)


def widen(source, ref):
    for part in range(ref.shape[0]):
        ref[part] = source[:, part * LANES : (part + 1) * LANES].astype(F32)


def pack(ref, out):
    for part in range(ref.shape[0]):
        out[:, part * LANES : (part + 1) * LANES] = ref[part].astype(BF16)


def project(normed, weights, first, mask, e32, gating):
    row_count, columns = mask.shape
    hidden = e32.shape[1] // (2 * row_count)
    projected = jnp.dot(weights, normed, preferred_element_type=F32)
    for at in range(0, normed.shape[1], LANES):
        row, column = divmod(first + at, columns)
        block = projected[:, at : at + LANES]
        kept = mask[row : row + 1, column : column + LANES]
        for side in range(2):
            low = 2 * hidden * side
            values = block[low + hidden : low + 2 * hidden] * kept
            values = (jnp.tanh(block[low : low + hidden]) + 1.0) * values
            rows = pl.ds(side * row_count + row, hidden, stride=2 * row_count)
            e32[column // LANES, rows, :] = values
        gating[:, first + at : first + at + LANES] = jnp.tanh(block[4 * hidden :]) + 1.0


def start_kernel(
    pair_h, mask_h, chain_h, embed_h, gain_h, bias_h, gain_oh, bias_oh, left_h, right_h, gate_h,
    out, state, gating, mask_out, columns_out,
    pair, mask, chain, small, weights, e32, rows, arrived,
):
    row_count, columns, channels = pair.shape
    moves = [(pair_h.at[row], pair.at[row], 0) for row in range(row_count)]
    smalls = (embed_h, gain_h, bias_h, gain_oh, bias_oh)
    moves += [(source, small.at[place], 1) for place, source in enumerate(smalls)]
    moves += [(chain_h, chain, 2)]
    hidden = weights.shape[2]
    for place, source in enumerate((left_h, left_h, right_h, right_h, gate_h)):
        lanes = pl.ds(place % 2 * hidden, hidden)
        moves += [(source.at[0, :, lanes], weights.at[place], 3)]
    moves += [(mask_h, mask, 4)]
    for source, target, which in moves:
        pltpu.make_async_copy(source, target, arrived.at[which]).start()
    first = lax.axis_index(AXES) * row_count
    one = unit(1.0)

    def wait(whole, which):
        pltpu.make_async_copy(whole, whole, arrived.at[which]).wait()

    wait(small, 1)
    wait(chain, 2)
    wait(pair, 0)
    for place in range(4):
        rows[2 * place : 2 * place + 2, :] = small[(3, 4, 1, 2)[place]]
    turned = jnp.transpose(rows[...])
    columns_out[...] = turned
    gain_c, bias_c = spread(turned[:, 4:5]), spread(turned[:, 6:7])
    rows[0:2, :] = small[0]
    turned = jnp.transpose(rows[...])
    other, same = spread(turned[:, 0:1]), spread(turned[:, 1:2])
    chains = jnp.broadcast_to(chain[...].astype(F32), (row_count, chain.shape[1]))
    place = lax.broadcasted_iota(jnp.int32, chains.shape, 1)
    mine = first + lax.broadcasted_iota(jnp.int32, chains.shape, 0)
    own = jnp.sum(jnp.where(place == mine, chains, 0.0), axis=1, keepdims=True)
    alike = jnp.where(chains == own, 1.0, 0.0)
    normed = []
    for begin in range(0, row_count * columns, LANES):
        row, column = divmod(begin, columns)
        values = lax.dot_general(
            one, pair[row, column : column + LANES, :], ON_LANES, preferred_element_type=F32
        )
        hit = jnp.broadcast_to(alike[row : row + 1, column : column + LANES], values.shape)
        values = values + jnp.where(hit > 0.5, same, other)
        state[:, begin : begin + LANES] = values
        normed.append(normalize(values, gain_c, bias_c))
    wait(weights, 3)
    wait(mask, 4)
    mask_out[...] = mask[...].astype(F32) * 0.5
    turned = turn_all([weights[place] for place in range(weights.shape[0])])
    for place in range(0, len(normed), 2):
        pair_of = jnp.concatenate(normed[place : place + 2], axis=1)
        project(pair_of, turned, place * LANES, mask_out, e32, gating)
    pack(e32, out)


def apart(low, high, half):
    upper = lax.broadcasted_iota(jnp.int32, low.shape, 1) < half
    firsts = jnp.where(upper, low, pltpu.roll(high, half, 1))
    return firsts, jnp.where(upper, pltpu.roll(low, half, 1), high)


def product_kernel(incoming, row_count, x, out):
    columns = x.shape[1]
    devices = columns // row_count
    per_device = out.shape[0] // columns
    sources = x.shape[0] // (per_device * 2 * row_count)
    tiles = x[...].astype(F32).reshape(sources // 2, 2, per_device, 2 * row_count, columns)
    products = []
    for channel in range(per_device):
        sides = apart(tiles[:, 0, channel], tiles[:, 1, channel], row_count)
        left, right = (
            side.reshape(sources * row_count, columns).astype(BF16) for side in sides
        )
        products.append(
            lax.dot_general(
                left, right, ON_SUBLANES if incoming else ON_LANES, preferred_element_type=F32
            ).reshape(devices // 2, 2 * row_count, columns)
        )
    if per_device == 1:
        out[...] = products[0].reshape(columns, columns).astype(BF16)
        return
    even, odd = [], []
    for channel in range(0, per_device, 2):
        low, high = apart(products[channel], products[channel + 1], row_count)
        even.append(low)
        odd.append(high)
    merged = jnp.stack([jnp.stack(even, axis=1), jnp.stack(odd, axis=1)], axis=1)
    out[...] = merged.reshape(out.shape).astype(BF16)


def finish(y32, first, lanes, columns, gain, bias, weight):
    row_count = y32.shape[1] // gain.shape[0]
    normed = []
    for at in range(first, first + lanes, LANES):
        row, column = divmod(at, columns)
        rows = pl.ds(row, gain.shape[0], stride=row_count)
        normed.append(normalize(y32[column // LANES, rows, :], gain, bias))
    return jnp.dot(weight, jnp.concatenate(normed, axis=1), preferred_element_type=F32)


def middle_kernel(
    y, state, gating, mask, turned, weight_o, left, right, gate,
    out, state_out, gating_out, y32, e32,
):
    row_count, columns = mask.shape
    gain_o, bias_o = spread(turned[:, 0:1]), spread(turned[:, 2:3])
    gain, bias = spread(turned[:, 5:6]), spread(turned[:, 7:8])
    weight = jnp.transpose(weight_o[0] * 0.5)
    weights = turn_all(halves(left[1], right[1], gate[1]))
    widen(y, y32)
    for at in range(0, row_count * columns, 2 * LANES):
        lanes = slice(at, at + 2 * LANES)
        update = finish(y32, at, 2 * LANES, columns, gain_o, bias_o, weight)
        stored = (state[:, lanes] + gating[:, lanes] * update).astype(BF16)
        state_out[:, lanes] = stored
        values = stored.astype(F32)
        normed = [normalize(values[:, q : q + LANES], gain, bias) for q in (0, LANES)]
        project(jnp.concatenate(normed, axis=1), weights, at, mask, e32, gating_out)
    pack(e32, out)


def end_kernel(y, state, gating, turned, weight_o, out, y32):
    row_count, columns, channels = out.shape
    gain_o, bias_o = spread(turned[:, 1:2]), spread(turned[:, 3:4])
    weight = jnp.transpose(weight_o[1] * 0.5)
    half = y.shape[0] // 2
    for part in range(y32.shape[0]):
        lanes = slice(part * LANES, (part + 1) * LANES)
        y32[part] = y[:half, lanes].astype(F32) + y[half:, lanes].astype(F32)
    update = finish(y32, 0, row_count * columns, columns, gain_o, bias_o, weight)
    stored = (state[...].astype(F32) + gating[...] * update).astype(BF16)
    for row in range(row_count):
        lanes = slice(row * columns, (row + 1) * columns)
        out[row] = jnp.transpose(stored[:, lanes])


def call(kernel, shapes, scratch, semaphores=0, far_in=False):
    near = pl.BlockSpec(memory_space=pltpu.VMEM)
    far = pl.BlockSpec(memory_space=pltpu.HBM)

    def run(*operands):
        if far_in:
            operands = [pltpu.with_memory_space_constraint(o, pltpu.HBM) for o in operands]
        return pl.pallas_call(
            kernel,
            out_shape=[jax.ShapeDtypeStruct(*s) for s in shapes],
            in_specs=[far if far_in else near] * len(operands),
            out_specs=[near] * len(shapes),
            scratch_shapes=[pltpu.VMEM(*s) for s in scratch]
            + [pltpu.SemaphoreType.DMA((semaphores,))] * (semaphores > 0),
            compiler_params=pltpu.CompilerParams(vmem_limit_bytes=16 << 20),
        )(*operands)

    return run


def exchange(rows, halves=1):
    devices = lax.axis_size(AXES[0]) * lax.axis_size(AXES[1])
    part = devices // halves
    groups = None
    if halves > 1:
        groups = [list(range(at, at + part)) for at in range(0, devices, part)]
    count, columns = rows.shape
    moved = lax.all_to_all(
        rows.reshape(part, count // part, columns),
        AXES,
        split_axis=0,
        concat_axis=0,
        tiled=True,
        axis_index_groups=groups,
    )
    return moved.reshape(count, columns)


def shards(
    pair_repr,
    pair_mask,
    chain_index,
    entity_embed,
    input_gain,
    input_bias,
    left_weight,
    right_weight,
    gate_weight,
    output_gain,
    output_bias,
    output_weight,
):
    row_count, columns, channels = pair_repr.shape
    hidden = output_weight.shape[1]
    devices = lax.axis_size(AXES[0]) * lax.axis_size(AXES[1])
    positions = row_count * columns
    edge = (hidden * 2 * row_count, columns)
    prod = (hidden * row_count, columns)
    wide = (channels, positions)

    def tall(shape):
        return ((shape[1] // LANES, shape[0], LANES), F32)

    columnar = ((channels, 8), F32)

    sent, state, gating, mask, turned = call(
        start_kernel,
        [(edge, BF16), (wide, F32), (wide, F32), (pair_mask.shape, F32), columnar],
        [(pair_repr.shape, BF16), (pair_mask.shape, jnp.int32), ((1, columns), jnp.int32)]
        + [((5, 2, channels), F32), ((5, channels, hidden), BF16), tall(edge), ((8, channels), F32)],
        semaphores=5,
        far_in=True,
    )(
        pair_repr, pair_mask, chain_index.reshape(1, -1), entity_embed, input_gain, input_bias,
        output_gain, output_bias, left_weight, right_weight, gate_weight,
    )

    def product(rows, incoming, halves):
        return call(
            functools.partial(product_kernel, incoming, row_count),
            [((prod[0] * halves, columns), BF16)],
            [],
        )(rows)[0]

    back = exchange(product(exchange(sent), False, 1))
    sent, state, gating = call(
        middle_kernel,
        [(edge, BF16), (wide, BF16), (wide, F32)],
        [tall(prod), tall(edge)],
    )(back, state, gating, mask, turned, output_weight, left_weight, right_weight, gate_weight)
    back = exchange(product(exchange(sent, 2), True, 2))
    return call(
        end_kernel,
        [(pair_repr.shape, BF16)],
        [tall(prod)],
    )(back, state, gating, turned, output_weight)[0]


def solution(mesh):
    rows = P(AXES, None)
    placed = (P(AXES, None, None), rows) + (P(),) * 10
    return jax.shard_map(
        shards, mesh=mesh, in_specs=placed, out_specs=P(AXES, None, None), check_vma=False
    )
```

```python
import functools

import jax
import jax.numpy as jnp
from jax import lax
from jax.experimental import pallas as pl
from jax.experimental.pallas import tpu as pltpu
from jax.sharding import PartitionSpec as P

AXES = ("grp", "blk")
F32, BF16 = jnp.float32, jnp.bfloat16
ON_SUBLANES = (((0,), (0,)), ((), ()))
ON_LANES = (((1,), (1,)), ((), ()))
LANES = 128


def unit(scale):
    down = lax.broadcasted_iota(jnp.int32, (LANES, LANES), 0)
    across = lax.broadcasted_iota(jnp.int32, (LANES, LANES), 1)
    return jnp.where(down == across, scale, 0.0).astype(BF16)


def turn(one, block):
    parts = [
        lax.dot_general(
            one, block[:, at : at + LANES], ON_LANES, preferred_element_type=F32
        ).astype(BF16)
        for at in range(0, block.shape[1], LANES)
    ]
    return jnp.concatenate(parts)


def turn_all(parts):
    scaled = [part if place in (1, 3) else part * 0.5 for place, part in enumerate(parts)]
    return jnp.transpose(jnp.concatenate(scaled, axis=1))


def halves(left, right, gate):
    hidden = left.shape[-1] // 2
    return [
        left[..., :hidden], left[..., hidden:], right[..., :hidden], right[..., hidden:], gate
    ]


def spread(column):
    return jnp.broadcast_to(column, (column.shape[0], LANES))


def normalize(values, gain, bias):
    average = jnp.mean(values, axis=0, keepdims=True)
    centered = values - average
    variance = jnp.mean(centered * centered, axis=0, keepdims=True)
    return (centered * lax.rsqrt(variance + 1e-05) * gain + bias).astype(BF16)


def put(ref, first, count, stride, values):
    for part in range(ref.shape[0]):
        at = part * LANES
        ref[part, pl.ds(first, count, stride=stride), :] = values[:, at : at + LANES]


def take(ref, first, count, stride):
    rows = pl.ds(first, count, stride=stride)
    return jnp.concatenate([ref[part, rows, :] for part in range(ref.shape[0])], axis=1)


def widen(source, ref):
    for part in range(ref.shape[0]):
        ref[part] = source[:, part * LANES : (part + 1) * LANES].astype(F32)


def pack(ref, out):
    for part in range(ref.shape[0]):
        out[:, part * LANES : (part + 1) * LANES] = ref[part].astype(BF16)


def project(normed, weights, first, mask, e32, gating):
    row_count, columns = mask.shape
    hidden = e32.shape[1] // (2 * row_count)
    projected = jnp.dot(weights, normed, preferred_element_type=F32)
    for at in range(0, normed.shape[1], LANES):
        row, column = divmod(first + at, columns)
        block = projected[:, at : at + LANES]
        kept = mask[row : row + 1, column : column + LANES]
        for side in range(2):
            low = 2 * hidden * side
            values = block[low + hidden : low + 2 * hidden] * kept
            values = (jnp.tanh(block[low : low + hidden]) + 1.0) * values
            rows = pl.ds(side * row_count + row, hidden, stride=2 * row_count)
            e32[column // LANES, rows, :] = values
        gating[:, first + at : first + at + LANES] = jnp.tanh(block[4 * hidden :]) + 1.0


def start_kernel(
    pair_h, mask_h, chain_h, embed_h, gain_h, bias_h, gain_oh, bias_oh, left_h, right_h, gate_h,
    out, state, gating, mask_out, columns_out,
    pair, mask, chain, small, weights, e32, rows, arrived,
):
    row_count, columns, channels = pair.shape
    moves = [(pair_h.at[row], pair.at[row], 0) for row in range(row_count)]
    smalls = (embed_h, gain_h, bias_h, gain_oh, bias_oh)
    moves += [(source, small.at[place], 1) for place, source in enumerate(smalls)]
    moves += [(chain_h, chain, 2)]
    hidden = weights.shape[2]
    for place, source in enumerate((left_h, left_h, right_h, right_h, gate_h)):
        lanes = pl.ds(place % 2 * hidden, hidden)
        moves += [(source.at[0, :, lanes], weights.at[place], 3)]
    moves += [(mask_h, mask, 4)]
    for source, target, which in moves:
        pltpu.make_async_copy(source, target, arrived.at[which]).start()
    first = lax.axis_index(AXES) * row_count
    one = unit(1.0)

    def wait(whole, which):
        pltpu.make_async_copy(whole, whole, arrived.at[which]).wait()

    wait(small, 1)
    wait(chain, 2)
    wait(pair, 0)
    for place in range(4):
        rows[2 * place : 2 * place + 2, :] = small[(3, 4, 1, 2)[place]]
    turned = jnp.transpose(rows[...])
    columns_out[...] = turned
    gain_c, bias_c = spread(turned[:, 4:5]), spread(turned[:, 6:7])
    rows[0:2, :] = small[0]
    turned = jnp.transpose(rows[...])
    other, same = spread(turned[:, 0:1]), spread(turned[:, 1:2])
    chains = jnp.broadcast_to(chain[...].astype(F32), (row_count, chain.shape[1]))
    place = lax.broadcasted_iota(jnp.int32, chains.shape, 1)
    mine = first + lax.broadcasted_iota(jnp.int32, chains.shape, 0)
    own = jnp.sum(jnp.where(place == mine, chains, 0.0), axis=1, keepdims=True)
    alike = jnp.where(chains == own, 1.0, 0.0)
    normed = []
    for begin in range(0, row_count * columns, LANES):
        row, column = divmod(begin, columns)
        values = lax.dot_general(
            one, pair[row, column : column + LANES, :], ON_LANES, preferred_element_type=F32
        )
        hit = jnp.broadcast_to(alike[row : row + 1, column : column + LANES], values.shape)
        values = values + jnp.where(hit > 0.5, same, other)
        state[:, begin : begin + LANES] = values
        normed.append(normalize(values, gain_c, bias_c))
    wait(weights, 3)
    wait(mask, 4)
    mask_out[...] = mask[...].astype(F32) * 0.5
    turned = turn_all([weights[place] for place in range(weights.shape[0])])
    for place in range(0, len(normed), 2):
        pair_of = jnp.concatenate(normed[place : place + 2], axis=1)
        project(pair_of, turned, place * LANES, mask_out, e32, gating)
    pack(e32, out)


def apart(low, high, half):
    upper = lax.broadcasted_iota(jnp.int32, low.shape, 1) < half
    firsts = jnp.where(upper, low, pltpu.roll(high, half, 1))
    return firsts, jnp.where(upper, pltpu.roll(low, half, 1), high)


def product_kernel(incoming, devices, x, out):
    columns = x.shape[1]
    row_count = columns // devices
    per_device = x.shape[0] // (2 * columns)
    tiles = x[...].astype(F32).reshape(devices // 2, 2, per_device, 2 * row_count, columns)
    products = []
    for channel in range(per_device):
        sides = apart(tiles[:, 0, channel], tiles[:, 1, channel], row_count)
        left, right = (side.reshape(columns, columns).astype(BF16) for side in sides)
        products.append(
            lax.dot_general(
                left, right, ON_SUBLANES if incoming else ON_LANES, preferred_element_type=F32
            ).reshape(devices // 2, 2 * row_count, columns)
        )
    if per_device == 1:
        out[...] = products[0].reshape(columns, columns).astype(BF16)
        return
    even, odd = [], []
    for channel in range(0, per_device, 2):
        low, high = apart(products[channel], products[channel + 1], row_count)
        even.append(low)
        odd.append(high)
    merged = jnp.stack([jnp.stack(even, axis=1), jnp.stack(odd, axis=1)], axis=1)
    out[...] = merged.reshape(out.shape).astype(BF16)


def finish(y32, first, lanes, columns, gain, bias, weight):
    row_count = y32.shape[1] // gain.shape[0]
    normed = []
    for at in range(first, first + lanes, LANES):
        row, column = divmod(at, columns)
        rows = pl.ds(row, gain.shape[0], stride=row_count)
        normed.append(normalize(y32[column // LANES, rows, :], gain, bias))
    return jnp.dot(weight, jnp.concatenate(normed, axis=1), preferred_element_type=F32)


def middle_kernel(
    y, state, gating, mask, turned, weight_o, left, right, gate,
    out, state_out, gating_out, y32, e32,
):
    row_count, columns = mask.shape
    gain_o, bias_o = spread(turned[:, 0:1]), spread(turned[:, 2:3])
    gain, bias = spread(turned[:, 5:6]), spread(turned[:, 7:8])
    weight = jnp.transpose(weight_o[0] * 0.5)
    weights = turn_all(halves(left[1], right[1], gate[1]))
    widen(y, y32)
    for at in range(0, row_count * columns, 2 * LANES):
        lanes = slice(at, at + 2 * LANES)
        update = finish(y32, at, 2 * LANES, columns, gain_o, bias_o, weight)
        stored = (state[:, lanes] + gating[:, lanes] * update).astype(BF16)
        state_out[:, lanes] = stored
        values = stored.astype(F32)
        normed = [normalize(values[:, q : q + LANES], gain, bias) for q in (0, LANES)]
        project(jnp.concatenate(normed, axis=1), weights, at, mask, e32, gating_out)
    pack(e32, out)


def end_kernel(y, state, gating, turned, weight_o, out, y32, ready, written):
    row_count, columns, channels = out.shape
    gain_o, bias_o = spread(turned[:, 1:2]), spread(turned[:, 3:4])
    weight = jnp.transpose(weight_o[1] * 0.5)
    widen(y, y32)
    update = finish(y32, 0, row_count * columns, columns, gain_o, bias_o, weight)
    stored = (state[...].astype(F32) + gating[...] * update).astype(BF16)
    for row in range(row_count):
        lanes = slice(row * columns, (row + 1) * columns)
        ready[row] = jnp.transpose(stored[:, lanes])
        if row % 1 == 1 - 1:
            done = pl.ds(row - 1 + 1, 1)
            pltpu.make_async_copy(ready.at[done], out.at[done], written.at[0]).start()
    pltpu.make_async_copy(ready, out, written.at[0]).wait()


def call(kernel, shapes, scratch, semaphores=0, far_in=False, far_out=False):
    near = pl.BlockSpec(memory_space=pltpu.VMEM)
    far = pl.BlockSpec(memory_space=pltpu.HBM)

    def run(*operands):
        if far_in:
            operands = [pltpu.with_memory_space_constraint(o, pltpu.HBM) for o in operands]
        return pl.pallas_call(
            kernel,
            out_shape=[jax.ShapeDtypeStruct(*s) for s in shapes],
            in_specs=[far if far_in else near] * len(operands),
            out_specs=[far if far_out else near] * len(shapes),
            scratch_shapes=[pltpu.VMEM(*s) for s in scratch]
            + [pltpu.SemaphoreType.DMA((semaphores,))] * (semaphores > 0),
            compiler_params=pltpu.CompilerParams(vmem_limit_bytes=16 << 20),
        )(*operands)

    return run


def exchange(rows):
    devices = lax.axis_size(AXES[0]) * lax.axis_size(AXES[1])
    count, columns = rows.shape
    moved = lax.all_to_all(
        rows.reshape(devices, count // devices, columns),
        AXES,
        split_axis=0,
        concat_axis=0,
        tiled=True,
    )
    return moved.reshape(count, columns)


def shards(
    pair_repr,
    pair_mask,
    chain_index,
    entity_embed,
    input_gain,
    input_bias,
    left_weight,
    right_weight,
    gate_weight,
    output_gain,
    output_bias,
    output_weight,
):
    row_count, columns, channels = pair_repr.shape
    hidden = output_weight.shape[1]
    devices = lax.axis_size(AXES[0]) * lax.axis_size(AXES[1])
    positions = row_count * columns
    edge = (hidden * 2 * row_count, columns)
    prod = (hidden * row_count, columns)
    wide = (channels, positions)

    def tall(shape):
        return ((shape[1] // LANES, shape[0], LANES), F32)

    columnar = ((channels, 8), F32)

    sent, state, gating, mask, turned = call(
        start_kernel,
        [(edge, BF16), (wide, F32), (wide, F32), (pair_mask.shape, F32), columnar],
        [(pair_repr.shape, BF16), (pair_mask.shape, jnp.int32), ((1, columns), jnp.int32)]
        + [((5, 2, channels), F32), ((5, channels, hidden), BF16), tall(edge), ((8, channels), F32)],
        semaphores=5,
        far_in=True,
    )(
        pair_repr, pair_mask, chain_index.reshape(1, -1), entity_embed, input_gain, input_bias,
        output_gain, output_bias, left_weight, right_weight, gate_weight,
    )

    def product(rows, incoming):
        return call(
            functools.partial(product_kernel, incoming, devices),
            [(prod, BF16)],
            [],
        )(rows)[0]

    back = exchange(product(exchange(sent), False))
    sent, state, gating = call(
        middle_kernel,
        [(edge, BF16), (wide, BF16), (wide, F32)],
        [tall(prod), tall(edge)],
    )(back, state, gating, mask, turned, output_weight, left_weight, right_weight, gate_weight)
    back = exchange(product(exchange(sent), True))
    return call(
        end_kernel,
        [(pair_repr.shape, BF16)],
        [tall(prod), (pair_repr.shape, BF16)],
        semaphores=1,
        far_out=True,
    )(back, state, gating, turned, output_weight)[0]


def solution(mesh):
    rows = P(AXES, None)
    placed = (P(AXES, None, None), rows) + (P(),) * 10
    return jax.shard_map(
        shards, mesh=mesh, in_specs=placed, out_specs=P(AXES, None, None), check_vma=False
    )
```

```python
import functools

import jax
import jax.numpy as jnp
from jax import lax
from jax.experimental import pallas as pl
from jax.experimental.pallas import tpu as pltpu
from jax.sharding import PartitionSpec as P

AXES = ("grp", "blk")
F32, BF16 = jnp.float32, jnp.bfloat16
ON_SUBLANES = (((0,), (0,)), ((), ()))
ON_LANES = (((1,), (1,)), ((), ()))
LANES = 128


def unit(scale):
    down = lax.broadcasted_iota(jnp.int32, (LANES, LANES), 0)
    across = lax.broadcasted_iota(jnp.int32, (LANES, LANES), 1)
    return jnp.where(down == across, scale, 0.0).astype(BF16)


def turn(one, block):
    parts = [
        lax.dot_general(
            one, block[:, at : at + LANES], ON_LANES, preferred_element_type=F32
        ).astype(BF16)
        for at in range(0, block.shape[1], LANES)
    ]
    return jnp.concatenate(parts)


def turn_all(parts):
    scaled = [part if place in (1, 3) else part * 0.5 for place, part in enumerate(parts)]
    return jnp.transpose(jnp.concatenate(scaled, axis=1))


def halves(left, right):
    hidden = left.shape[-1] // 2
    return [
        left[..., :hidden], left[..., hidden:], right[..., :hidden], right[..., hidden:]
    ]


def spread(column):
    return jnp.broadcast_to(column, (column.shape[0], LANES))


def normalize(values, gain, bias):
    average = jnp.mean(values, axis=0, keepdims=True)
    centered = values - average
    variance = jnp.mean(centered * centered, axis=0, keepdims=True)
    return (centered * lax.rsqrt(variance + 1e-05) * gain + bias).astype(BF16)


def put(ref, first, count, stride, values):
    for part in range(ref.shape[0]):
        at = part * LANES
        ref[part, pl.ds(first, count, stride=stride), :] = values[:, at : at + LANES]


def take(ref, first, count, stride):
    rows = pl.ds(first, count, stride=stride)
    return jnp.concatenate([ref[part, rows, :] for part in range(ref.shape[0])], axis=1)


def widen(source, ref):
    for part in range(ref.shape[0]):
        ref[part] = source[:, part * LANES : (part + 1) * LANES].astype(F32)


def pack(ref, out):
    for part in range(ref.shape[0]):
        out[:, part * LANES : (part + 1) * LANES] = ref[part].astype(BF16)


def project(normed, weights, first, mask, e32):
    row_count, columns = mask.shape
    hidden = e32.shape[1] // (2 * row_count)
    projected = jnp.dot(weights, normed, preferred_element_type=F32)
    for at in range(0, normed.shape[1], LANES):
        row, column = divmod(first + at, columns)
        block = projected[:, at : at + LANES]
        kept = mask[row : row + 1, column : column + LANES]
        for side in range(2):
            low = 2 * hidden * side
            values = block[low + hidden : low + 2 * hidden] * kept
            values = (jnp.tanh(block[low : low + hidden]) + 1.0) * values
            rows = pl.ds(side * row_count + row, hidden, stride=2 * row_count)
            e32[column // LANES, rows, :] = values


def start_kernel(
    pair_h, mask_h, chain_h, embed_h, gain_h, bias_h, gain_oh, bias_oh, left_h, right_h,
    out, state, normed_out, mask_out, columns_out,
    pair, mask, chain, small, weights, e32, rows, arrived,
):
    row_count, columns, channels = pair.shape
    moves = [(pair_h.at[row], pair.at[row], 0) for row in range(row_count)]
    smalls = (embed_h, gain_h, bias_h, gain_oh, bias_oh)
    moves += [(source, small.at[place], 1) for place, source in enumerate(smalls)]
    moves += [(chain_h, chain, 2)]
    hidden = weights.shape[2]
    for place, source in enumerate((left_h, left_h, right_h, right_h)):
        lanes = pl.ds(place % 2 * hidden, hidden)
        moves += [(source.at[0, :, lanes], weights.at[place], 3)]
    moves += [(mask_h, mask, 4)]
    for source, target, which in moves:
        pltpu.make_async_copy(source, target, arrived.at[which]).start()
    first = lax.axis_index(AXES) * row_count
    one = unit(1.0)

    def wait(whole, which):
        pltpu.make_async_copy(whole, whole, arrived.at[which]).wait()

    wait(small, 1)
    wait(chain, 2)
    wait(pair, 0)
    for place in range(4):
        rows[2 * place : 2 * place + 2, :] = small[(3, 4, 1, 2)[place]]
    turned = jnp.transpose(rows[...])
    columns_out[...] = turned
    gain_c, bias_c = spread(turned[:, 4:5]), spread(turned[:, 6:7])
    rows[0:2, :] = small[0]
    turned = jnp.transpose(rows[...])
    other, same = spread(turned[:, 0:1]), spread(turned[:, 1:2])
    chains = jnp.broadcast_to(chain[...].astype(F32), (row_count, chain.shape[1]))
    place = lax.broadcasted_iota(jnp.int32, chains.shape, 1)
    mine = first + lax.broadcasted_iota(jnp.int32, chains.shape, 0)
    own = jnp.sum(jnp.where(place == mine, chains, 0.0), axis=1, keepdims=True)
    alike = jnp.where(chains == own, 1.0, 0.0)
    normed = []
    for begin in range(0, row_count * columns, LANES):
        row, column = divmod(begin, columns)
        values = lax.dot_general(
            one, pair[row, column : column + LANES, :], ON_LANES, preferred_element_type=F32
        )
        hit = jnp.broadcast_to(alike[row : row + 1, column : column + LANES], values.shape)
        values = values + jnp.where(hit > 0.5, same, other)
        state[:, begin : begin + LANES] = values
        normed.append(normalize(values, gain_c, bias_c))
    wait(weights, 3)
    wait(mask, 4)
    mask_out[...] = mask[...].astype(F32) * 0.5
    turned = turn_all([weights[place] for place in range(weights.shape[0])])
    for place in range(0, len(normed), 2):
        pair_of = jnp.concatenate(normed[place : place + 2], axis=1)
        normed_out[:, place * LANES : (place + 2) * LANES] = pair_of
        project(pair_of, turned, place * LANES, mask_out, e32)
    pack(e32, out)


def apart(low, high, half):
    upper = lax.broadcasted_iota(jnp.int32, low.shape, 1) < half
    firsts = jnp.where(upper, low, pltpu.roll(high, half, 1))
    return firsts, jnp.where(upper, pltpu.roll(low, half, 1), high)


def product_kernel(block_index, devices, x, normed, gate, out, gating):
    weight = jnp.transpose(gate[block_index] * 0.5)
    gating[...] = jnp.tanh(jnp.dot(weight, normed[...], preferred_element_type=F32)) + 1.0
    columns = x.shape[1]
    row_count = columns // devices
    per_device = x.shape[0] // (2 * columns)
    tiles = x[...].astype(F32).reshape(devices // 2, 2, per_device, 2 * row_count, columns)
    products = []
    for channel in range(per_device):
        sides = apart(tiles[:, 0, channel], tiles[:, 1, channel], row_count)
        left, right = (side.reshape(columns, columns).astype(BF16) for side in sides)
        products.append(
            lax.dot_general(
                left, right, ON_SUBLANES if block_index else ON_LANES, preferred_element_type=F32
            ).reshape(devices // 2, 2 * row_count, columns)
        )
    if per_device == 1:
        out[...] = products[0].reshape(columns, columns).astype(BF16)
        return
    even, odd = [], []
    for channel in range(0, per_device, 2):
        low, high = apart(products[channel], products[channel + 1], row_count)
        even.append(low)
        odd.append(high)
    merged = jnp.stack([jnp.stack(even, axis=1), jnp.stack(odd, axis=1)], axis=1)
    out[...] = merged.reshape(out.shape).astype(BF16)


def finish(y32, first, lanes, columns, gain, bias, weight):
    row_count = y32.shape[1] // gain.shape[0]
    normed = []
    for at in range(first, first + lanes, LANES):
        row, column = divmod(at, columns)
        rows = pl.ds(row, gain.shape[0], stride=row_count)
        normed.append(normalize(y32[column // LANES, rows, :], gain, bias))
    return jnp.dot(weight, jnp.concatenate(normed, axis=1), preferred_element_type=F32)


def middle_kernel(
    y, state, gating, mask, turned, weight_o, left, right,
    out, state_out, normed_out, y32, e32,
):
    row_count, columns = mask.shape
    gain_o, bias_o = spread(turned[:, 0:1]), spread(turned[:, 2:3])
    gain, bias = spread(turned[:, 5:6]), spread(turned[:, 7:8])
    weight = jnp.transpose(weight_o[0] * 0.5)
    weights = turn_all(halves(left[1], right[1]))
    widen(y, y32)
    for at in range(0, row_count * columns, 2 * LANES):
        lanes = slice(at, at + 2 * LANES)
        update = finish(y32, at, 2 * LANES, columns, gain_o, bias_o, weight)
        stored = (state[:, lanes] + gating[:, lanes] * update).astype(BF16)
        state_out[:, lanes] = stored
        values = stored.astype(F32)
        normed = [normalize(values[:, q : q + LANES], gain, bias) for q in (0, LANES)]
        flat = jnp.concatenate(normed, axis=1)
        normed_out[:, lanes] = flat
        project(flat, weights, at, mask, e32)
    pack(e32, out)


def end_kernel(y, state, gating, turned, weight_o, out, y32):
    row_count, columns, channels = out.shape
    gain_o, bias_o = spread(turned[:, 1:2]), spread(turned[:, 3:4])
    weight = jnp.transpose(weight_o[1] * 0.5)
    widen(y, y32)
    update = finish(y32, 0, row_count * columns, columns, gain_o, bias_o, weight)
    stored = (state[...].astype(F32) + gating[...] * update).astype(BF16)
    for row in range(row_count):
        lanes = slice(row * columns, (row + 1) * columns)
        out[row] = jnp.transpose(stored[:, lanes])


def call(kernel, shapes, scratch, semaphores=0, far_in=False):
    near = pl.BlockSpec(memory_space=pltpu.VMEM)
    far = pl.BlockSpec(memory_space=pltpu.HBM)

    def run(*operands):
        if far_in:
            operands = [pltpu.with_memory_space_constraint(o, pltpu.HBM) for o in operands]
        return pl.pallas_call(
            kernel,
            out_shape=[jax.ShapeDtypeStruct(*s) for s in shapes],
            in_specs=[far if far_in else near] * len(operands),
            out_specs=[near] * len(shapes),
            scratch_shapes=[pltpu.VMEM(*s) for s in scratch]
            + [pltpu.SemaphoreType.DMA((semaphores,))] * (semaphores > 0),
            compiler_params=pltpu.CompilerParams(vmem_limit_bytes=16 << 20),
        )(*operands)

    return run


def exchange(rows):
    devices = lax.axis_size(AXES[0]) * lax.axis_size(AXES[1])
    count, columns = rows.shape
    moved = lax.all_to_all(
        rows.reshape(devices, count // devices, columns),
        AXES,
        split_axis=0,
        concat_axis=0,
        tiled=True,
    )
    return moved.reshape(count, columns)


def shards(
    pair_repr,
    pair_mask,
    chain_index,
    entity_embed,
    input_gain,
    input_bias,
    left_weight,
    right_weight,
    gate_weight,
    output_gain,
    output_bias,
    output_weight,
):
    row_count, columns, channels = pair_repr.shape
    hidden = output_weight.shape[1]
    devices = lax.axis_size(AXES[0]) * lax.axis_size(AXES[1])
    positions = row_count * columns
    edge = (hidden * 2 * row_count, columns)
    prod = (hidden * row_count, columns)
    wide = (channels, positions)

    def tall(shape):
        return ((shape[1] // LANES, shape[0], LANES), F32)

    columnar = ((channels, 8), F32)

    sent, state, normed, mask, turned = call(
        start_kernel,
        [(edge, BF16), (wide, F32), (wide, BF16), (pair_mask.shape, F32), columnar],
        [(pair_repr.shape, BF16), (pair_mask.shape, jnp.int32), ((1, columns), jnp.int32)]
        + [((5, 2, channels), F32), ((4, channels, hidden), BF16), tall(edge), ((8, channels), F32)],
        semaphores=5,
        far_in=True,
    )(
        pair_repr, pair_mask, chain_index.reshape(1, -1), entity_embed, input_gain, input_bias,
        output_gain, output_bias, left_weight, right_weight,
    )

    def product(rows, block_index, normed):
        return call(
            functools.partial(product_kernel, block_index, devices),
            [(prod, BF16), (wide, F32)],
            [],
        )(rows, normed, gate_weight)

    back, gating = product(exchange(sent), 0, normed)
    back = exchange(back)
    sent, state, normed = call(
        middle_kernel,
        [(edge, BF16), (wide, BF16), (wide, BF16)],
        [tall(prod), tall(edge)],
    )(back, state, gating, mask, turned, output_weight, left_weight, right_weight)
    back, gating = product(exchange(sent), 1, normed)
    back = exchange(back)
    return call(
        end_kernel,
        [(pair_repr.shape, BF16)],
        [tall(prod)],
    )(back, state, gating, turned, output_weight)[0]


def solution(mesh):
    rows = P(AXES, None)
    placed = (P(AXES, None, None), rows) + (P(),) * 10
    return jax.shard_map(
        shards, mesh=mesh, in_specs=placed, out_specs=P(AXES, None, None), check_vma=False
    )
```

```python
import functools

import jax
import jax.numpy as jnp
from jax import lax
from jax.experimental import pallas as pl
from jax.experimental.pallas import tpu as pltpu
from jax.sharding import PartitionSpec as P

AXES = ("grp", "blk")
F32, BF16 = jnp.float32, jnp.bfloat16
ON_SUBLANES = (((0,), (0,)), ((), ()))
ON_LANES = (((1,), (1,)), ((), ()))
LANES = 128


def unit(scale):
    down = lax.broadcasted_iota(jnp.int32, (LANES, LANES), 0)
    across = lax.broadcasted_iota(jnp.int32, (LANES, LANES), 1)
    return jnp.where(down == across, scale, 0.0).astype(BF16)


def turn(one, block):
    parts = [
        lax.dot_general(
            one, block[:, at : at + LANES], ON_LANES, preferred_element_type=F32
        ).astype(BF16)
        for at in range(0, block.shape[1], LANES)
    ]
    return jnp.concatenate(parts)


def turn_all(parts):
    scaled = [part if place in (1, 3) else part * 0.5 for place, part in enumerate(parts)]
    return jnp.transpose(jnp.concatenate(scaled, axis=1))


def halves(left, right):
    hidden = left.shape[-1] // 2
    return [
        left[..., :hidden], left[..., hidden:], right[..., :hidden], right[..., hidden:]
    ]


def spread(column):
    return jnp.broadcast_to(column, (column.shape[0], LANES))


def normalize(values, gain, bias):
    average = jnp.mean(values, axis=0, keepdims=True)
    centered = values - average
    variance = jnp.mean(centered * centered, axis=0, keepdims=True)
    return (centered * lax.rsqrt(variance + 1e-05) * gain + bias).astype(BF16)


def put(ref, first, count, stride, values):
    for part in range(ref.shape[0]):
        at = part * LANES
        ref[part, pl.ds(first, count, stride=stride), :] = values[:, at : at + LANES]


def take(ref, first, count, stride):
    rows = pl.ds(first, count, stride=stride)
    return jnp.concatenate([ref[part, rows, :] for part in range(ref.shape[0])], axis=1)


def widen(source, ref):
    for part in range(ref.shape[0]):
        ref[part] = source[:, part * LANES : (part + 1) * LANES].astype(F32)


def pack(ref, out):
    for part in range(ref.shape[0]):
        out[:, part * LANES : (part + 1) * LANES] = ref[part].astype(BF16)


def project(normed, weights, first, mask, e32):
    row_count, columns = mask.shape
    hidden = e32.shape[1] // (2 * row_count)
    projected = jnp.dot(weights, normed, preferred_element_type=F32)
    for at in range(0, normed.shape[1], LANES):
        row, column = divmod(first + at, columns)
        block = projected[:, at : at + LANES]
        kept = mask[row : row + 1, column : column + LANES]
        for side in range(2):
            low = 2 * hidden * side
            values = block[low + hidden : low + 2 * hidden] * kept
            values = (jnp.tanh(block[low : low + hidden]) + 1.0) * values
            rows = pl.ds(side * row_count + row, hidden, stride=2 * row_count)
            e32[column // LANES, rows, :] = values


def start_kernel(
    pair_h, mask_h, chain_h, embed_h, gain_h, bias_h, gain_oh, bias_oh, left_h, right_h,
    out, state, normed_out, mask_out, columns_out,
    pair, mask, chain, small, weights, e32, rows, arrived,
):
    row_count, columns, channels = pair.shape
    moves = [(pair_h.at[row], pair.at[row], 0) for row in range(row_count)]
    smalls = (embed_h, gain_h, bias_h, gain_oh, bias_oh)
    moves += [(source, small.at[place], 1) for place, source in enumerate(smalls)]
    moves += [(chain_h, chain, 2)]
    hidden = weights.shape[2]
    for place, source in enumerate((left_h, left_h, right_h, right_h)):
        lanes = pl.ds(place % 2 * hidden, hidden)
        moves += [(source.at[0, :, lanes], weights.at[place], 3)]
    moves += [(mask_h, mask, 4)]
    for source, target, which in moves:
        pltpu.make_async_copy(source, target, arrived.at[which]).start()
    first = lax.axis_index(AXES) * row_count
    one = unit(1.0)

    def wait(whole, which):
        pltpu.make_async_copy(whole, whole, arrived.at[which]).wait()

    wait(small, 1)
    wait(chain, 2)
    wait(pair, 0)
    for place in range(4):
        rows[2 * place : 2 * place + 2, :] = small[(3, 4, 1, 2)[place]]
    turned = jnp.transpose(rows[...])
    columns_out[...] = turned
    gain_c, bias_c = spread(turned[:, 4:5]), spread(turned[:, 6:7])
    rows[0:2, :] = small[0]
    turned = jnp.transpose(rows[...])
    other, same = spread(turned[:, 0:1]), spread(turned[:, 1:2])
    chains = jnp.broadcast_to(chain[...].astype(F32), (row_count, chain.shape[1]))
    place = lax.broadcasted_iota(jnp.int32, chains.shape, 1)
    mine = first + lax.broadcasted_iota(jnp.int32, chains.shape, 0)
    own = jnp.sum(jnp.where(place == mine, chains, 0.0), axis=1, keepdims=True)
    alike = jnp.where(chains == own, 1.0, 0.0)
    normed = []
    for begin in range(0, row_count * columns, LANES):
        row, column = divmod(begin, columns)
        values = lax.dot_general(
            one, pair[row, column : column + LANES, :], ON_LANES, preferred_element_type=F32
        )
        hit = jnp.broadcast_to(alike[row : row + 1, column : column + LANES], values.shape)
        values = values + jnp.where(hit > 0.5, same, other)
        state[:, begin : begin + LANES] = values
        normed.append(normalize(values, gain_c, bias_c))
    wait(weights, 3)
    wait(mask, 4)
    mask_out[...] = mask[...].astype(F32) * 0.5
    turned = turn_all([weights[place] for place in range(weights.shape[0])])
    for place in range(0, len(normed), 2):
        pair_of = jnp.concatenate(normed[place : place + 2], axis=1)
        normed_out[:, place * LANES : (place + 2) * LANES] = pair_of
        project(pair_of, turned, place * LANES, mask_out, e32)
    pack(e32, out)


def apart(low, high, half):
    upper = lax.broadcasted_iota(jnp.int32, low.shape, 1) < half
    firsts = jnp.where(upper, low, pltpu.roll(high, half, 1))
    return firsts, jnp.where(upper, pltpu.roll(low, half, 1), high)


def product_kernel(block_index, devices, x, normed, gate, out, gating):
    weight = jnp.transpose(gate[block_index] * 0.5)
    gating[...] = jnp.tanh(jnp.dot(weight, normed[...], preferred_element_type=F32)) + 1.0
    columns = x.shape[1]
    row_count = columns // devices
    per_device = x.shape[0] // (2 * columns)
    tiles = x[...].astype(F32).reshape(devices // 2, 2, per_device, 2 * row_count, columns)
    products = []
    for channel in range(per_device):
        sides = apart(tiles[:, 0, channel], tiles[:, 1, channel], row_count)
        left, right = (side.reshape(columns, columns).astype(BF16) for side in sides)
        products.append(
            lax.dot_general(
                left, right, ON_SUBLANES if block_index else ON_LANES, preferred_element_type=F32
            ).reshape(devices // 2, 2 * row_count, columns)
        )
    if per_device == 1:
        out[...] = products[0].reshape(columns, columns).astype(BF16)
        return
    even, odd = [], []
    for channel in range(0, per_device, 2):
        low, high = apart(products[channel], products[channel + 1], row_count)
        even.append(low)
        odd.append(high)
    merged = jnp.stack([jnp.stack(even, axis=1), jnp.stack(odd, axis=1)], axis=1)
    out[...] = merged.reshape(out.shape).astype(BF16)


def finish(y32, first, lanes, columns, gain, bias, weight):
    row_count = y32.shape[1] // gain.shape[0]
    normed = []
    for at in range(first, first + lanes, LANES):
        row, column = divmod(at, columns)
        rows = pl.ds(row, gain.shape[0], stride=row_count)
        normed.append(normalize(y32[column // LANES, rows, :], gain, bias))
    return jnp.dot(weight, jnp.concatenate(normed, axis=1), preferred_element_type=F32)


def middle_kernel(
    y, state, gating, mask, turned, weight_o, left, right,
    out, state_out, normed_out, y32, e32,
):
    row_count, columns = mask.shape
    gain_o, bias_o = spread(turned[:, 0:1]), spread(turned[:, 2:3])
    gain, bias = spread(turned[:, 5:6]), spread(turned[:, 7:8])
    weight = jnp.transpose(weight_o[0] * 0.5)
    weights = turn_all(halves(left[1], right[1]))
    widen(y, y32)
    for at in range(0, row_count * columns, 2 * LANES):
        lanes = slice(at, at + 2 * LANES)
        update = finish(y32, at, 2 * LANES, columns, gain_o, bias_o, weight)
        stored = (state[:, lanes] + gating[:, lanes] * update).astype(BF16)
        state_out[:, lanes] = stored
        values = stored.astype(F32)
        normed = [normalize(values[:, q : q + LANES], gain, bias) for q in (0, LANES)]
        flat = jnp.concatenate(normed, axis=1)
        normed_out[:, lanes] = flat
        project(flat, weights, at, mask, e32)
    pack(e32, out)


def end_kernel(y, state, gating, turned, weight_o, out, y32, ready, written):
    row_count, columns, channels = out.shape
    gain_o, bias_o = spread(turned[:, 1:2]), spread(turned[:, 3:4])
    weight = jnp.transpose(weight_o[1] * 0.5)
    widen(y, y32)
    update = finish(y32, 0, row_count * columns, columns, gain_o, bias_o, weight)
    stored = (state[...].astype(F32) + gating[...] * update).astype(BF16)
    for row in range(row_count):
        lanes = slice(row * columns, (row + 1) * columns)
        ready[row] = jnp.transpose(stored[:, lanes])
        if row % 1 == 1 - 1:
            done = pl.ds(row - 1 + 1, 1)
            pltpu.make_async_copy(ready.at[done], out.at[done], written.at[0]).start()
    pltpu.make_async_copy(ready, out, written.at[0]).wait()


def call(kernel, shapes, scratch, semaphores=0, far_in=False, far_out=False):
    near = pl.BlockSpec(memory_space=pltpu.VMEM)
    far = pl.BlockSpec(memory_space=pltpu.HBM)

    def run(*operands):
        if far_in:
            operands = [pltpu.with_memory_space_constraint(o, pltpu.HBM) for o in operands]
        return pl.pallas_call(
            kernel,
            out_shape=[jax.ShapeDtypeStruct(*s) for s in shapes],
            in_specs=[far if far_in else near] * len(operands),
            out_specs=[far if far_out else near] * len(shapes),
            scratch_shapes=[pltpu.VMEM(*s) for s in scratch]
            + [pltpu.SemaphoreType.DMA((semaphores,))] * (semaphores > 0),
            compiler_params=pltpu.CompilerParams(vmem_limit_bytes=16 << 20),
        )(*operands)

    return run


def exchange(rows):
    devices = lax.axis_size(AXES[0]) * lax.axis_size(AXES[1])
    count, columns = rows.shape
    moved = lax.all_to_all(
        rows.reshape(devices, count // devices, columns),
        AXES,
        split_axis=0,
        concat_axis=0,
        tiled=True,
    )
    return moved.reshape(count, columns)


def shards(
    pair_repr,
    pair_mask,
    chain_index,
    entity_embed,
    input_gain,
    input_bias,
    left_weight,
    right_weight,
    gate_weight,
    output_gain,
    output_bias,
    output_weight,
):
    row_count, columns, channels = pair_repr.shape
    hidden = output_weight.shape[1]
    devices = lax.axis_size(AXES[0]) * lax.axis_size(AXES[1])
    positions = row_count * columns
    edge = (hidden * 2 * row_count, columns)
    prod = (hidden * row_count, columns)
    wide = (channels, positions)

    def tall(shape):
        return ((shape[1] // LANES, shape[0], LANES), F32)

    columnar = ((channels, 8), F32)

    sent, state, normed, mask, turned = call(
        start_kernel,
        [(edge, BF16), (wide, F32), (wide, BF16), (pair_mask.shape, F32), columnar],
        [(pair_repr.shape, BF16), (pair_mask.shape, jnp.int32), ((1, columns), jnp.int32)]
        + [((5, 2, channels), F32), ((4, channels, hidden), BF16), tall(edge), ((8, channels), F32)],
        semaphores=5,
        far_in=True,
    )(
        pair_repr, pair_mask, chain_index.reshape(1, -1), entity_embed, input_gain, input_bias,
        output_gain, output_bias, left_weight, right_weight,
    )

    def product(rows, block_index, normed):
        return call(
            functools.partial(product_kernel, block_index, devices),
            [(prod, BF16), (wide, F32)],
            [],
        )(rows, normed, gate_weight)

    back, gating = product(exchange(sent), 0, normed)
    back = exchange(back)
    sent, state, normed = call(
        middle_kernel,
        [(edge, BF16), (wide, BF16), (wide, BF16)],
        [tall(prod), tall(edge)],
    )(back, state, gating, mask, turned, output_weight, left_weight, right_weight)
    back, gating = product(exchange(sent), 1, normed)
    back = exchange(back)
    return call(
        end_kernel,
        [(pair_repr.shape, BF16)],
        [tall(prod), (pair_repr.shape, BF16)],
        semaphores=1,
        far_out=True,
    )(back, state, gating, turned, output_weight)[0]


def solution(mesh):
    rows = P(AXES, None)
    placed = (P(AXES, None, None), rows) + (P(),) * 10
    return jax.shard_map(
        shards, mesh=mesh, in_specs=placed, out_specs=P(AXES, None, None), check_vma=False
    )
```

```python
import functools

import jax
import jax.numpy as jnp
from jax import lax
from jax.experimental import pallas as pl
from jax.experimental.pallas import tpu as pltpu
from jax.sharding import PartitionSpec as P

AXES = ("grp", "blk")
F32, BF16 = jnp.float32, jnp.bfloat16
ON_SUBLANES = (((0,), (0,)), ((), ()))
ON_LANES = (((1,), (1,)), ((), ()))
LANES = 128


def unit(scale):
    down = lax.broadcasted_iota(jnp.int32, (LANES, LANES), 0)
    across = lax.broadcasted_iota(jnp.int32, (LANES, LANES), 1)
    return jnp.where(down == across, scale, 0.0).astype(BF16)


def turn(one, block):
    parts = [
        lax.dot_general(
            one, block[:, at : at + LANES], ON_LANES, preferred_element_type=F32
        ).astype(BF16)
        for at in range(0, block.shape[1], LANES)
    ]
    return jnp.concatenate(parts)


def turn_all(parts):
    scaled = [part if place in (1, 3) else part * 0.5 for place, part in enumerate(parts)]
    return jnp.transpose(jnp.concatenate(scaled, axis=1))


def halves(left, right):
    hidden = left.shape[-1] // 2
    return [
        left[..., :hidden], left[..., hidden:], right[..., :hidden], right[..., hidden:]
    ]


def spread(column):
    return jnp.broadcast_to(column, (column.shape[0], LANES))


def normalize(values, gain, bias):
    average = jnp.mean(values, axis=0, keepdims=True)
    centered = values - average
    variance = jnp.mean(centered * centered, axis=0, keepdims=True)
    return (centered * lax.rsqrt(variance + 1e-05) * gain + bias).astype(BF16)


def put(ref, first, count, stride, values):
    for part in range(ref.shape[0]):
        at = part * LANES
        ref[part, pl.ds(first, count, stride=stride), :] = values[:, at : at + LANES]


def take(ref, first, count, stride):
    rows = pl.ds(first, count, stride=stride)
    return jnp.concatenate([ref[part, rows, :] for part in range(ref.shape[0])], axis=1)


def widen(source, ref):
    for part in range(ref.shape[0]):
        ref[part] = source[:, part * LANES : (part + 1) * LANES].astype(F32)


def pack(ref, out):
    for part in range(ref.shape[0]):
        out[:, part * LANES : (part + 1) * LANES] = ref[part].astype(BF16)


def project(normed, weights, first, mask, e32):
    row_count, columns = mask.shape
    hidden = e32.shape[1] // (2 * row_count)
    projected = jnp.dot(weights, normed, preferred_element_type=F32)
    for at in range(0, normed.shape[1], LANES):
        row, column = divmod(first + at, columns)
        block = projected[:, at : at + LANES]
        kept = mask[row : row + 1, column : column + LANES]
        for side in range(2):
            low = 2 * hidden * side
            values = block[low + hidden : low + 2 * hidden] * kept
            values = (jnp.tanh(block[low : low + hidden]) + 1.0) * values
            rows = pl.ds(side * row_count + row, hidden, stride=2 * row_count)
            e32[column // LANES, rows, :] = values


def start_kernel(
    pair_h, mask_h, chain_h, embed_h, gain_h, bias_h, gain_oh, bias_oh, left_h, right_h,
    out, state, normed_out, mask_out, columns_out,
    pair, mask, chain, small, weights, e32, rows, arrived,
):
    row_count, columns, channels = pair.shape
    moves = [(pair_h.at[row], pair.at[row], 0) for row in range(row_count)]
    smalls = (embed_h, gain_h, bias_h, gain_oh, bias_oh)
    moves += [(source, small.at[place], 1) for place, source in enumerate(smalls)]
    moves += [(chain_h, chain, 2)]
    hidden = weights.shape[2]
    for place, source in enumerate((left_h, left_h, right_h, right_h)):
        lanes = pl.ds(place % 2 * hidden, hidden)
        moves += [(source.at[0, :, lanes], weights.at[place], 3)]
    moves += [(mask_h, mask, 4)]
    for source, target, which in moves:
        pltpu.make_async_copy(source, target, arrived.at[which]).start()
    first = lax.axis_index(AXES) * row_count
    one = unit(1.0)

    def wait(whole, which):
        pltpu.make_async_copy(whole, whole, arrived.at[which]).wait()

    wait(small, 1)
    wait(chain, 2)
    wait(pair, 0)
    for place in range(4):
        rows[2 * place : 2 * place + 2, :] = small[(3, 4, 1, 2)[place]]
    turned = jnp.transpose(rows[...])
    columns_out[...] = turned
    gain_c, bias_c = spread(turned[:, 4:5]), spread(turned[:, 6:7])
    rows[0:2, :] = small[0]
    turned = jnp.transpose(rows[...])
    other, same = spread(turned[:, 0:1]), spread(turned[:, 1:2])
    chains = jnp.broadcast_to(chain[...].astype(F32), (row_count, chain.shape[1]))
    place = lax.broadcasted_iota(jnp.int32, chains.shape, 1)
    mine = first + lax.broadcasted_iota(jnp.int32, chains.shape, 0)
    own = jnp.sum(jnp.where(place == mine, chains, 0.0), axis=1, keepdims=True)
    alike = jnp.where(chains == own, 1.0, 0.0)
    normed = []
    for begin in range(0, row_count * columns, LANES):
        row, column = divmod(begin, columns)
        values = lax.dot_general(
            one, pair[row, column : column + LANES, :], ON_LANES, preferred_element_type=F32
        )
        hit = jnp.broadcast_to(alike[row : row + 1, column : column + LANES], values.shape)
        values = values + jnp.where(hit > 0.5, same, other)
        state[:, begin : begin + LANES] = values
        normed.append(normalize(values, gain_c, bias_c))
    wait(weights, 3)
    wait(mask, 4)
    mask_out[...] = mask[...].astype(F32) * 0.5
    turned = turn_all([weights[place] for place in range(weights.shape[0])])
    for place in range(0, len(normed), 2):
        pair_of = jnp.concatenate(normed[place : place + 2], axis=1)
        normed_out[:, place * LANES : (place + 2) * LANES] = pair_of
        project(pair_of, turned, place * LANES, mask_out, e32)
    pack(e32, out)


def apart(low, high, half):
    upper = lax.broadcasted_iota(jnp.int32, low.shape, 1) < half
    firsts = jnp.where(upper, low, pltpu.roll(high, half, 1))
    return firsts, jnp.where(upper, pltpu.roll(low, half, 1), high)


def product_kernel(block_index, devices, x, normed, gate, out, gating):
    weight = jnp.transpose(gate[block_index] * 0.5)
    gating[...] = jnp.tanh(jnp.dot(weight, normed[...], preferred_element_type=F32)) + 1.0
    columns = x.shape[1]
    row_count = columns // devices
    per_device = x.shape[0] // (2 * columns)
    tiles = x[...].astype(F32).reshape(devices // 2, 2, per_device, 2 * row_count, columns)
    products = []
    for channel in range(per_device):
        sides = apart(tiles[:, 0, channel], tiles[:, 1, channel], row_count)
        left, right = (side.reshape(columns, columns).astype(BF16) for side in sides)
        products.append(
            lax.dot_general(
                left, right, ON_SUBLANES if block_index else ON_LANES, preferred_element_type=F32
            ).reshape(devices // 2, 2 * row_count, columns)
        )
    if per_device == 1:
        out[...] = products[0].reshape(columns, columns).astype(BF16)
        return
    even, odd = [], []
    for channel in range(0, per_device, 2):
        low, high = apart(products[channel], products[channel + 1], row_count)
        even.append(low)
        odd.append(high)
    merged = jnp.stack([jnp.stack(even, axis=1), jnp.stack(odd, axis=1)], axis=1)
    out[...] = merged.reshape(out.shape).astype(BF16)


def finish(y32, first, lanes, columns, gain, bias, weight):
    row_count = y32.shape[1] // gain.shape[0]
    normed = []
    for at in range(first, first + lanes, LANES):
        row, column = divmod(at, columns)
        rows = pl.ds(row, gain.shape[0], stride=row_count)
        normed.append(normalize(y32[column // LANES, rows, :], gain, bias))
    return jnp.dot(weight, jnp.concatenate(normed, axis=1), preferred_element_type=F32)


def middle_kernel(
    y, state, gating, mask, turned, weight_o, left, right,
    out, state_out, normed_out, y32, e32,
):
    row_count, columns = mask.shape
    gain_o, bias_o = spread(turned[:, 0:1]), spread(turned[:, 2:3])
    gain, bias = spread(turned[:, 5:6]), spread(turned[:, 7:8])
    weight = jnp.transpose(weight_o[0] * 0.5)
    weights = turn_all(halves(left[1], right[1]))
    widen(y, y32)
    for at in range(0, row_count * columns, 2 * LANES):
        lanes = slice(at, at + 2 * LANES)
        update = finish(y32, at, 2 * LANES, columns, gain_o, bias_o, weight)
        stored = (state[:, lanes] + gating[:, lanes] * update).astype(BF16)
        state_out[:, lanes] = stored
        values = stored.astype(F32)
        normed = [normalize(values[:, q : q + LANES], gain, bias) for q in (0, LANES)]
        flat = jnp.concatenate(normed, axis=1)
        normed_out[:, lanes] = flat
        project(flat, weights, at, mask, e32)
    pack(e32, out)


def end_kernel(y, state, gating, turned, weight_o, out, y32, ready, written):
    row_count, columns, channels = out.shape
    gain_o, bias_o = spread(turned[:, 1:2]), spread(turned[:, 3:4])
    weight = jnp.transpose(weight_o[1] * 0.5)
    widen(y, y32)
    update = finish(y32, 0, row_count * columns, columns, gain_o, bias_o, weight)
    stored = (state[...].astype(F32) + gating[...] * update).astype(BF16)
    for row in range(row_count):
        lanes = slice(row * columns, (row + 1) * columns)
        ready[row] = jnp.transpose(stored[:, lanes])
        if row % 1 == 1 - 1:
            done = pl.ds(row - 1 + 1, 1)
            pltpu.make_async_copy(ready.at[done], out.at[done], written.at[0]).start()
    pltpu.make_async_copy(ready, out, written.at[0]).wait()


def call(kernel, shapes, scratch, semaphores=0, far_in=False, far_out=False, flags=None):
    near = pl.BlockSpec(memory_space=pltpu.VMEM)
    far = pl.BlockSpec(memory_space=pltpu.HBM)

    def run(*operands):
        if far_in:
            operands = [pltpu.with_memory_space_constraint(o, pltpu.HBM) for o in operands]
        return pl.pallas_call(
            kernel,
            out_shape=[jax.ShapeDtypeStruct(*s) for s in shapes],
            in_specs=[far if far_in else near] * len(operands),
            out_specs=[far if far_out else near] * len(shapes),
            scratch_shapes=[pltpu.VMEM(*s) for s in scratch]
            + [pltpu.SemaphoreType.DMA((semaphores,))] * (semaphores > 0),
            compiler_params=pltpu.CompilerParams(vmem_limit_bytes=16 << 20, flags=flags),
        )(*operands)

    return run


def exchange(rows):
    devices = lax.axis_size(AXES[0]) * lax.axis_size(AXES[1])
    count, columns = rows.shape
    moved = lax.all_to_all(
        rows.reshape(devices, count // devices, columns),
        AXES,
        split_axis=0,
        concat_axis=0,
        tiled=True,
    )
    return moved.reshape(count, columns)


def shards(
    pair_repr,
    pair_mask,
    chain_index,
    entity_embed,
    input_gain,
    input_bias,
    left_weight,
    right_weight,
    gate_weight,
    output_gain,
    output_bias,
    output_weight,
):
    row_count, columns, channels = pair_repr.shape
    hidden = output_weight.shape[1]
    devices = lax.axis_size(AXES[0]) * lax.axis_size(AXES[1])
    positions = row_count * columns
    edge = (hidden * 2 * row_count, columns)
    prod = (hidden * row_count, columns)
    wide = (channels, positions)

    def tall(shape):
        return ((shape[1] // LANES, shape[0], LANES), F32)

    columnar = ((channels, 8), F32)

    sent, state, normed, mask, turned = call(
        start_kernel,
        [(edge, BF16), (wide, F32), (wide, BF16), (pair_mask.shape, F32), columnar],
        [(pair_repr.shape, BF16), (pair_mask.shape, jnp.int32), ((1, columns), jnp.int32)]
        + [((5, 2, channels), F32), ((4, channels, hidden), BF16), tall(edge), ((8, channels), F32)],
        semaphores=5,
        far_in=True,
    )(
        pair_repr, pair_mask, chain_index.reshape(1, -1), entity_embed, input_gain, input_bias,
        output_gain, output_bias, left_weight, right_weight,
    )

    def product(rows, block_index, normed):
        return call(
            functools.partial(product_kernel, block_index, devices),
            [(prod, BF16), (wide, F32)],
            [],
        )(rows, normed, gate_weight)

    back, gating = product(exchange(sent), 0, normed)
    back = exchange(back)
    sent, state, normed = call(
        middle_kernel,
        [(edge, BF16), (wide, BF16), (wide, BF16)],
        [tall(prod), tall(edge)],
    )(back, state, gating, mask, turned, output_weight, left_weight, right_weight)
    back, gating = product(exchange(sent), 1, normed)
    back = exchange(back)
    return call(
        end_kernel,
        [(pair_repr.shape, BF16)],
        [tall(prod), (pair_repr.shape, BF16)],
        semaphores=1,
        far_out=True,
    )(back, state, gating, turned, output_weight)[0]


def solution(mesh):
    rows = P(AXES, None)
    placed = (P(AXES, None, None), rows) + (P(),) * 10
    return jax.shard_map(
        shards, mesh=mesh, in_specs=placed, out_specs=P(AXES, None, None), check_vma=False
    )
```
